32 devices in a mesh: tile: 8 (over z, y), src: 4 (over x, core).
Axes of the slice: x: 2, y: 2, z: 4, core: 2. Of those that a mesh axis runs over, the one named last changes fastest.
Arguments:
- excitation: bfloat16 [2, 512, 8192], P(None, 'src', 'tile'), may hold values from -6 to 6
- near_blocks: bfloat16 [16, 3, 2, 512, 512], P('tile'), may hold values from -0.02734375 to 0.02734375
- source_basis: bfloat16 [16, 2, 24, 512], P('tile'), may hold values from -0.1875 to 0.1875
- target_basis: bfloat16 [16, 2, 24, 512], P('tile'), may hold values from -0.625 to 0.625
- coupling: bfloat16 [2, 384, 384], P(None, None, 'tile'), may hold values from -0.109375 to 0.109375
- pair_rank: int32 [16, 16], P(None, 'tile'), may hold values from 2 to 24
- far_link: int32 [16, 16], P(None, 'tile'), may hold values 0 or 1
- focal_kernel: bfloat16 [2, 64, 8192], P(None, None, 'tile'), may hold values from -0.046875 to 0.046875
- focal_target: float32 [64], replicated, may hold values from 0.3 to 0.9
- focal_owner: int32 [64], replicated, may hold values from 0 to 63, each once
Outputs:
- field: float32 [2, 512, 8192], P(None, 'src', 'tile')
- focal_residual: float32 [64], P('tile')
- adjoint: float32 [2, 512, 8192], P(None, 'src', 'tile')
The draws below stay inside these ranges and needn't reach their ends.
Inputs may be any that keep to these rules, and one draw needn't show every extreme that they name: `focal_owner`: each focal point has its own slot; slot k belongs to index k // 8 of tile.
All inputs are finite; a program needn't handle non-finite values. No bound on the sum of `far_link` on one device may be relied on, other than what follows from the above.
Results may differ from the reference program's by a relative error of at most 0.006.
Values may be sent and summed in bfloat16 or wider, within the bound.
No kernel may reach another device: no remote copies, remote signals or barrier semaphores. Data moves between devices by JAX's collectives and lax.ppermute only.
A program may use at most 64 MiB of HBM per device.

```python
import jax
import jax.numpy as jnp

TILE = 512
RANK = 24
TILES = 16
UNK = 8192
SOURCES = 512
FOCAL = 64


def plant(result, stream_key, low, top_value):
    spot = [jax.random.randint(jax.random.fold_in(stream_key, axis), (), 0, length) for axis, length in enumerate(result.shape)]
    widest = result.shape.index(max(result.shape))
    next_to = spot[:widest] + [(spot[widest] + 1) % result.shape[widest]] + spot[widest + 1:]
    return result.at[tuple(spot)].set(low).at[tuple(next_to)].set(top_value)


def steps_of(own_key, shape, shards, least, high):
    def one(position, shards_of):
        steps = jax.random.uniform(jax.random.fold_in(jax.random.fold_in(own_key, 6), position), (shards_of,), jnp.float32, least / len(shards), high / len(shards))
        return jnp.repeat(jnp.exp(steps), shape[position] // shards_of).reshape((-1,) + (1,) * (len(shape) - position - 1))

    gain = one(*shards[0])
    for cut in shards[1:]:
        gain = gain * one(*cut)
    return gain


def gaussian(rng, shape, deviation, limit, shards=(), kind=jnp.bfloat16):
    result = deviation * jax.random.normal(rng, shape, jnp.float32)
    if shards:
        result = result * steps_of(rng, shape, shards, -0.22, 0.18)
    return jnp.clip(result, -limit, limit).astype(kind)


def setup_inputs(seed: int = 0) -> dict:
    streams_of = jax.random.split(jax.random.key(seed), 11)
    return {
        "excitation": gaussian(streams_of[0], (2, SOURCES, UNK), 1.0, 6.0, ((1, 4), (2, 8))),
        "near_blocks": gaussian(streams_of[1], (TILES, 3, 2, TILE, TILE), (96 * TILE) ** -0.5, 0.02734375, ((0, 8),)),
        "source_basis": gaussian(streams_of[2], (TILES, 2, RANK, TILE), (2 * TILE) ** -0.5, 0.1875, ((0, 8),)),
        "target_basis": gaussian(streams_of[3], (TILES, 2, RANK, TILE), (4 * RANK) ** -0.5, 0.625, ((0, 8),)),
        "coupling": gaussian(streams_of[4], (2, TILES * RANK, TILES * RANK), (8 * TILES * RANK) ** -0.5, 0.109375, ((2, 8),)),
        "pair_rank": plant(jax.random.randint(streams_of[5], (TILES, TILES), 2, RANK + 1), jax.random.fold_in(streams_of[5], 1), 2, RANK).astype(jnp.int32),
        "far_link": plant((jax.random.randint(streams_of[6], (TILES, TILES), 0, 4) < 3).astype(jnp.int32), jax.random.fold_in(streams_of[6], 1), 0, 1),
        "focal_kernel": gaussian(streams_of[7], (2, FOCAL, UNK), (2 * UNK) ** -0.5, 0.046875, ((2, 8),)),
        "focal_target": jnp.clip(jax.random.uniform(streams_of[8], (FOCAL,), jnp.float32, 0.3, 0.9), 0.3, 0.9),
        "focal_owner": jax.random.permutation(streams_of[9], FOCAL).astype(jnp.int32),
    }


DAMPING = 0.8


def complex_einsum(formula, left, right):
    left = left.astype(jnp.float32)
    right = right.astype(jnp.float32)
    real_part = jnp.einsum(formula, left[0], right[0]) - jnp.einsum(formula, left[1], right[1])
    imag_part = jnp.einsum(formula, left[0], right[1]) + jnp.einsum(formula, left[1], right[0])
    return jnp.stack([real_part, imag_part])


def masked_coupling(coupling, pair_rank, far_link):
    tiles = pair_rank.shape[0]
    source_tiles = jnp.arange(tiles)[:, None]
    target_tiles = jnp.arange(tiles)[None, :]
    distance = (target_tiles - source_tiles) % tiles
    far_pairs = (far_link == 1) & (distance != 0) & (distance != 1) & (distance != tiles - 1)
    levels = jnp.arange(RANK)
    rank_limit = pair_rank[:, None, :, None]
    rank_mask = far_pairs[:, None, :, None] & (levels[None, :, None, None] < rank_limit) & (levels[None, None, None, :] < rank_limit)
    rank_mask = rank_mask.reshape(tiles * RANK, tiles * RANK)
    return coupling * rank_mask.astype(coupling.dtype)


def apply_forward(field, near_blocks, source_basis, target_basis, masked):
    rows = field.shape[1]
    field_bf = field.astype(jnp.bfloat16).reshape(2, rows, TILES, TILE)
    near_part = jnp.zeros((2, rows, TILES, TILE), jnp.float32)
    for offset in range(3):
        shifted = jnp.roll(field_bf, -(offset - 1), axis=2)
        blocks = jnp.moveaxis(near_blocks[:, offset], 1, 0)
        near_part = near_part + complex_einsum('stn,tnm->stm', shifted, blocks)
    source_moved = jnp.moveaxis(source_basis, 1, 0)
    target_moved = jnp.moveaxis(target_basis, 1, 0)
    coeff = complex_einsum('stn,trn->str', field_bf, source_moved).astype(jnp.bfloat16).reshape(2, rows, TILES * RANK)
    coupled = complex_einsum('sj,ji->si', coeff, masked).astype(jnp.bfloat16).reshape(2, rows, TILES, RANK)
    far_part = complex_einsum('str,trn->stn', coupled, target_moved)
    return field + (near_part + far_part).reshape(2, rows, TILES * TILE)


def apply_transpose(field, near_blocks, source_basis, target_basis, masked):
    rows = field.shape[1]
    field_bf = field.astype(jnp.bfloat16).reshape(2, rows, TILES, TILE)
    near_part = jnp.zeros((2, rows, TILES, TILE), jnp.float32)
    for offset in range(3):
        blocks = jnp.moveaxis(near_blocks[:, offset], 1, 0)
        moved = complex_einsum('sto,tio->sti', field_bf, blocks)
        near_part = near_part + jnp.roll(moved, offset - 1, axis=2)
    source_moved = jnp.moveaxis(source_basis, 1, 0)
    target_moved = jnp.moveaxis(target_basis, 1, 0)
    projected = complex_einsum('stn,trn->str', field_bf, target_moved).astype(jnp.bfloat16).reshape(2, rows, TILES * RANK)
    summed_back = complex_einsum('si,ji->sj', projected, masked).astype(jnp.bfloat16).reshape(2, rows, TILES, RANK)
    far_part = complex_einsum('str,trn->stn', summed_back, source_moved)
    return field + (near_part + far_part).reshape(2, rows, TILES * TILE)


def reference(excitation, near_blocks, source_basis, target_basis, coupling, pair_rank, far_link, focal_kernel, focal_target, focal_owner):
    masked = masked_coupling(coupling, pair_rank, far_link)
    right_side = excitation.astype(jnp.float32)
    field = right_side
    for update in range(2):
        field = field + DAMPING * (right_side - apply_forward(field, near_blocks, source_basis, target_basis, masked))
    focal = complex_einsum('sn,fn->sf', field.astype(jnp.bfloat16), focal_kernel)
    intensity = jnp.sum(focal[0] * focal[0] + focal[1] * focal[1], axis=0)
    sources = focal.shape[1]
    residual_part = jnp.tanh(intensity / (2.0 * sources)) - focal_target
    weights = jnp.stack([residual_part * focal[0], -residual_part * focal[1]]).astype(jnp.bfloat16)
    scale_factor = (TILES * TILE / FOCAL) ** 0.5
    source_term = complex_einsum('sf,fn->sn', weights, focal_kernel) * scale_factor
    adjoint = source_term + DAMPING * (source_term - apply_transpose(source_term, near_blocks, source_basis, target_basis, masked))
    focal_residual = jnp.zeros((FOCAL,), jnp.float32).at[focal_owner].set(residual_part)
    return field, focal_residual, adjoint
```

```python
import functools

import jax
import jax.numpy as jnp
from jax import lax
from jax.experimental import pallas as pl
from jax.experimental.pallas import tpu as pltpu
from jax.sharding import PartitionSpec as P

DAMPING = 0.8
F32 = jnp.float32
BF16 = jnp.bfloat16


def nn(a, b):
    return lax.dot_general(a, b, (((1,), (0,)), ((), ())), preferred_element_type=F32)


def nt(a, b):
    return lax.dot_general(a, b, (((1,), (1,)), ((), ())), preferred_element_type=F32)


def tn(a, b):
    return lax.dot_general(a, b, (((0,), (0,)), ((), ())), preferred_element_type=F32)


def rows_join(p, q):
    h = p.shape[0] // 2
    return jnp.concatenate([p[:h] - q[h:], p[h:] + q[:h]], axis=0)


def lanes_join(p, q):
    h = p.shape[1] // 2
    return jnp.concatenate([p[:, :h] - q[:, h:], p[:, h:] + q[:, :h]], axis=1)


def lanes_turn(x):
    h = x.shape[1] // 2
    return jnp.concatenate([-x[:, h:], x[:, :h]], axis=1)


def stacked(x):
    return x.reshape(x.shape[0] * x.shape[1], x.shape[2])


def project(basis, field, tile):
    tc = basis.shape[0]
    parts = []
    for i in range(tc):
        v = field[:, i * tile : (i + 1) * tile]
        parts.append(lanes_join(nt(basis[i, 0], v), nt(basis[i, 1], v)))
    return jnp.concatenate(parts, axis=0)


def expand(coeff_t, basis, i):
    rank = basis.shape[2]
    c = coeff_t[i * rank : (i + 1) * rank]
    return tn(c.astype(BF16), basis[i, 0]) + tn(lanes_turn(c).astype(BF16), basis[i, 1])


def first_kernel(first_ref, e_ref, s_ref, t_ref, k_ref, c_ref, pr_ref, fl_ref, out_ref, m_ref):
    tiles, tc = pr_ref.shape
    rank, tile = s_ref.shape[2:]
    lanes = tc * rank
    n = out_ref.shape[0]
    width = out_ref.shape[2]
    rows = 2 * e_ref.shape[1]
    j = lax.broadcasted_iota(jnp.int32, (tiles, tc), 0)
    i = lax.broadcasted_iota(jnp.int32, (tiles, tc), 1) + first_ref[0, 0]
    distance = i - j
    distance = jnp.where(distance < 0, distance + tiles, distance)
    far = (fl_ref[...] == 1) & (distance != 0) & (distance != 1) & (distance != tiles - 1)
    limit = jnp.where(far, pr_ref[...], 0)
    lane = lax.broadcasted_iota(jnp.int32, (tiles, lanes), 1)
    level = lax.broadcasted_iota(jnp.int32, (rank, lanes), 1)
    wide = jnp.broadcast_to(limit[:, 0:1], (tiles, lanes))
    for a in range(1, tc):
        wide = jnp.where(lane >= a * rank, limit[:, a : a + 1], wide)
        level = jnp.where(level >= rank, level - rank, level)
    above = lax.broadcasted_iota(jnp.int32, (rank, lanes), 0)
    top = jnp.maximum(above, level)
    mask = jnp.concatenate(
        [jnp.where(top < wide[a : a + 1], 1.0, 0.0).astype(F32) for a in range(tiles)], axis=0
    )
    m_re = (c_ref[0].astype(F32) * mask).astype(BF16)
    m_im = (c_ref[1].astype(F32) * mask).astype(BF16)
    m_ref[0] = m_re
    m_ref[1] = m_im
    coeff = project(s_ref, stacked(e_ref[...]), tile).astype(BF16)
    proj = project(t_ref, stacked(k_ref[...]), tile)
    back = nn(m_re, proj.astype(BF16)) + nn(m_im, lanes_turn(proj).astype(BF16))
    for d in range(n):
        out_ref[d, :, 0:rows] = coeff
        out_ref[d, :, rows:width] = back[d * lanes : (d + 1) * lanes].astype(BF16)


def kernel_side(k_ref, nb_ref, loc_ref, gl_ref, gr_ref):
    tc, _, _, tile, _ = nb_ref.shape
    k = stacked(k_ref[...])

    def moved(i, o):
        own = k[:, i * tile : (i + 1) * tile]
        return rows_join(nt(own, nb_ref[i, o, 0]), nt(own, nb_ref[i, o, 1]))

    gl_ref[...] = moved(0, 0).astype(BF16)
    gr_ref[...] = moved(tc - 1, 2).astype(BF16)
    for m in range(tc):
        total = None
        for o in range(3):
            i = m + 1 - o
            if 0 <= i < tc:
                part = moved(i, o)
                total = part if total is None else total + part
        loc_ref[:, m * tile : (m + 1) * tile] = total


def near_inside(v_ref, nb_ref, loc_ref):
    tc, _, _, tile, _ = nb_ref.shape
    v = v_ref[...]
    for i in range(tc):
        p = q = None
        for o in range(3):
            j = i + o - 1
            if 0 <= j < tc:
                own = v[:, j * tile : (j + 1) * tile]
                pp, qq = nn(own, nb_ref[i, o, 0]), nn(own, nb_ref[i, o, 1])
                p, q = (pp, qq) if p is None else (p + pp, q + qq)
        loc_ref[:, i * tile : (i + 1) * tile] = rows_join(p, q)


def applied(i, near_ref, hl_ref, hr_ref, nb_ref, coupled, t_ref):
    tc, _, _, tile, _ = nb_ref.shape
    total = near_ref[:, i * tile : (i + 1) * tile] + expand(coupled, t_ref, i)
    if i == 0:
        total = total + rows_join(nn(hl_ref[...], nb_ref[0, 0, 0]), nn(hl_ref[...], nb_ref[0, 0, 1]))
    if i == tc - 1:
        total = total + rows_join(nn(hr_ref[...], nb_ref[i, 2, 0]), nn(hr_ref[...], nb_ref[i, 2, 1]))
    return total


def coupled_of(gathered, m_ref):
    turned = lanes_turn(gathered)
    coupled = tn(m_ref[0], gathered) + tn(m_ref[1], turned)
    return coupled.astype(BF16).astype(F32)


def middle_kernel(
    e_ref, near_ref, hl_ref, hr_ref, nb_ref, got_ref, m_ref, s_ref, t_ref, k_ref, loc_ref, gl_ref, gr_ref,
    base_ref, f1_ref, fl_ref, fr_ref, out_ref, r_ref,
):
    tc, _, _, tile, _ = nb_ref.shape
    n, lanes, _ = got_ref.shape
    rows, width = f1_ref.shape
    focal2 = gl_ref.shape[0]
    focal = focal2 // 2
    e = stacked(e_ref[...])
    coupled = coupled_of(got_ref[:, :, 0:rows].reshape(n * lanes, rows), m_ref)
    mixes = []
    for i in range(tc):
        cut = slice(i * tile, (i + 1) * tile)
        start = e[:, cut].astype(F32)
        field = start - DAMPING * applied(i, near_ref, hl_ref, hr_ref, nb_ref, coupled, t_ref)
        rounded = field.astype(BF16)
        f1_ref[:, cut] = rounded
        if i == 0:
            fl_ref[...] = rounded
        if i == tc - 1:
            fr_ref[...] = rounded
        mix = (1.0 - DAMPING) * field + DAMPING * start
        base_ref[:, cut] = mix
        mixes.append(mix.astype(BF16))
    f1 = f1_ref[...]
    back = jnp.sum(got_ref[:, :, rows:].astype(F32), axis=0).astype(BF16).astype(F32)
    k = stacked(k_ref[...])
    r_ref[0:focal2] = k
    for i in range(tc):
        cut = slice(i * tile, (i + 1) * tile)
        total = loc_ref[:, cut] + expand(back, s_ref, i)
        if i == 0:
            total = total + gr_ref[...].astype(F32)
        if i == tc - 1:
            total = total + gl_ref[...].astype(F32)
        r_ref[focal2:, cut] = (-DAMPING * total).astype(BF16)
    p = nt(k, jnp.concatenate(mixes, axis=1)) + nt(r_ref[focal2:], f1)
    half = rows // 2
    part = jnp.concatenate(
        [p[:focal, :half] - p[focal:, half:], p[:focal, half:] + p[focal:, :half]], axis=1
    ).astype(BF16)
    coeff = project(s_ref, f1, tile).astype(BF16)
    for d in range(n):
        out_ref[d, 0:focal] = part
        out_ref[d, focal:] = coeff


def sum_kernel(got_ref, foc_ref, int_ref):
    focal = foc_ref.shape[0]
    half = foc_ref.shape[1] // 2
    foc = jnp.sum(got_ref[:, 0:focal].astype(F32), axis=0)
    foc_ref[...] = foc
    power = foc[:, :half] * foc[:, :half] + foc[:, half:] * foc[:, half:]
    column = jnp.sum(power, axis=1, keepdims=True)
    int_ref[...] = jnp.sum(jnp.where(eye(focal), column, 0.0), axis=0, keepdims=True)


def eye(n):
    return lax.broadcasted_iota(jnp.int32, (n, n), 0) == lax.broadcasted_iota(jnp.int32, (n, n), 1)


def last_kernel(first_ref, foc_ref, int_ref, target_ref, owner_ref, r_ref, adj_ref, res_ref, *, sources, scale):
    focal = foc_ref.shape[0]
    half = foc_ref.shape[1] // 2
    row = jnp.tanh(int_ref[...] / (2.0 * sources)) - target_ref[...]
    diagonal = eye(focal)
    column = jnp.sum(jnp.where(diagonal, row, 0.0), axis=1, keepdims=True)
    owner = jnp.sum(jnp.where(diagonal, owner_ref[...], 0), axis=1, keepdims=True)
    slots = res_ref.shape[1]
    slot = lax.broadcasted_iota(jnp.int32, (focal, slots), 1) + first_ref[0, 1]
    res_ref[...] = jnp.sum(jnp.where(owner == slot, column, 0.0), axis=0, keepdims=True)
    re = column * foc_ref[:, :half]
    im = -column * foc_ref[:, half:]
    w = jnp.concatenate([re, im], axis=1).astype(BF16)
    turned = jnp.concatenate([-im, re], axis=1).astype(BF16)
    out = scale * tn(jnp.concatenate([w, turned, w, turned], axis=0), r_ref[...])
    adj_ref[0] = out[:half]
    adj_ref[1] = out[half:]


def field_kernel(base_ref, near_ref, hl_ref, hr_ref, nb_ref, got_ref, m_ref, t_ref, out_ref):
    tc, _, _, tile, _ = nb_ref.shape
    n, total, rows = got_ref.shape
    lanes = m_ref.shape[2]
    half = rows // 2
    coupled = coupled_of(got_ref[:, total - lanes :].reshape(n * lanes, rows), m_ref)
    for i in range(tc):
        cut = slice(i * tile, (i + 1) * tile)
        field = base_ref[:, cut] - DAMPING * applied(i, near_ref, hl_ref, hr_ref, nb_ref, coupled, t_ref)
        out_ref[0, :, cut] = field[:half]
        out_ref[1, :, cut] = field[half:]


VM = pl.BlockSpec(memory_space=pltpu.VMEM)
SM = pl.BlockSpec(memory_space=pltpu.SMEM)


def call(kernel, name, outs, *args, scalars=0):
    return pl.pallas_call(
        kernel,
        out_shape=[jax.ShapeDtypeStruct(s, d) for s, d in outs],
        in_specs=[SM] * scalars + [VM] * (len(args) - scalars),
        out_specs=[VM] * len(outs),
        name=name,
    )(*args)


def per_device(e, nb, sb, tb, coupling, pair_rank, far_link, fk, target, owner):
    tc, _, _, tile, _ = nb.shape
    rank = sb.shape[2]
    lanes = tc * rank
    rows = 2 * e.shape[1]
    width = e.shape[2]
    tiles = pair_rank.shape[0]
    focal = target.shape[0]
    n = lax.axis_size("tile")
    slots = focal // n
    sources = e.shape[1] * lax.axis_size("src")
    up = [(i, (i + 1) % n) for i in range(n)]
    down = [(j, i) for i, j in up]

    def exchange(to_left, to_right):
        return lax.ppermute(to_right, "tile", up), lax.ppermute(to_left, "tile", down)

    here = lax.axis_index("tile")
    first = jnp.stack([here * tc, here * slots]).astype(jnp.int32)[None]
    flat = stacked(e)
    hl, hr = exchange(flat[:, :tile], flat[:, width - tile :])
    send, masked = call(
        first_kernel, "first",
        [((n, lanes, rows + 2 * focal), BF16), ((2, tiles * rank, lanes), BF16)],
        first, e, sb, tb, fk, coupling, pair_rank, far_link, scalars=1,
    )
    got = lax.all_to_all(send, "tile", split_axis=0, concat_axis=0, tiled=True)
    loc, gl, gr = call(
        kernel_side, "kernel_side",
        [((2 * focal, width), F32), ((2 * focal, tile), BF16), ((2 * focal, tile), BF16)],
        fk, nb,
    )
    from_left, from_right = exchange(gl, gr)
    (near,) = call(near_inside, "near_inside", [((rows, width), F32)], flat, nb)
    base, f1, fl, fr, send1, r4 = call(
        middle_kernel, "middle",
        [
            ((rows, width), F32),
            ((rows, width), BF16),
            ((rows, tile), BF16),
            ((rows, tile), BF16),
            ((n, focal + lanes, rows), BF16),
            ((4 * focal, width), BF16),
        ],
        e, near, hl, hr, nb, got, masked, sb, tb, fk, loc, from_right, from_left,
    )
    got1 = lax.all_to_all(send1, "tile", split_axis=0, concat_axis=0, tiled=True)
    hl1, hr1 = exchange(fl, fr)
    (near1,) = call(near_inside, "near_inside_again", [((rows, width), F32)], f1, nb)
    foc, part = call(sum_kernel, "focal_sum", [((focal, rows), F32), ((1, focal), F32)], got1)
    intensity = lax.psum(part, "src")
    adjoint, residual = call(
        functools.partial(last_kernel, sources=sources, scale=(tiles * tile / focal) ** 0.5),
        "adjoint",
        [((2, rows // 2, width), F32), ((1, slots), F32)],
        first, foc, intensity, target[None], owner[None], r4, scalars=1,
    )
    (field,) = call(
        field_kernel, "field", [((2, rows // 2, width), F32)],
        base, near1, hl1, hr1, nb, got1, masked, tb,
    )
    return field, residual[0], adjoint


def solution(mesh):
    return jax.shard_map(
        per_device,
        mesh=mesh,
        in_specs=(
            P(None, "src", "tile"),
            P("tile", None, None, None, None),
            P("tile", None, None, None),
            P("tile", None, None, None),
            P(None, None, "tile"),
            P(None, "tile"),
            P(None, "tile"),
            P(None, None, "tile"),
            P(),
            P(),
        ),
        out_specs=(P(None, "src", "tile"), P("tile"), P(None, "src", "tile")),
        check_vma=False,
    )
```

```python
import functools
import math

import jax
import jax.numpy as jnp
from jax import lax
from jax.experimental import pallas as pl
from jax.experimental.pallas import tpu as pltpu
from jax.sharding import PartitionSpec as P


DAMPING = 0.8
F32 = jnp.float32
BF16 = jnp.bfloat16


def nn(a, b):
    return lax.dot_general(a, b, (((1,), (0,)), ((), ())), preferred_element_type=F32)


def nt(a, b):
    return lax.dot_general(a, b, (((1,), (1,)), ((), ())), preferred_element_type=F32)


def tn(a, b):
    return lax.dot_general(a, b, (((0,), (0,)), ((), ())), preferred_element_type=F32)


def rows_join(p, q):
    h = p.shape[0] // 2
    return jnp.concatenate([p[:h] - q[h:], p[h:] + q[:h]], axis=0)


def lanes_join(p, q):
    h = p.shape[1] // 2
    return jnp.concatenate([p[:, :h] - q[:, h:], p[:, h:] + q[:, :h]], axis=1)


def lanes_turn(x):
    h = x.shape[1] // 2
    return jnp.concatenate([-x[:, h:], x[:, :h]], axis=1)


def stacked(x):
    return x.reshape(x.shape[0] * x.shape[1], x.shape[2])


class Operand:
    def __init__(self, copy, ref):
        self.copy, self.ref = copy, ref

    def get(self):
        if self.copy is not None:
            self.copy.wait()
            self.copy = None
        return self.ref

    def __getitem__(self, index):
        return self.get()[index]


class Blocks:
    def __init__(self, operands):
        self.operands = operands

    def __getitem__(self, index):
        return self.operands[index[:2]][index[2:] + (slice(None),) * (3 - len(index[2:]))]


class Result:
    def __init__(self, ref, out=None, sems=None):
        self.ref, self.out, self.sems, self.copies = ref, out, sems, []

    def send(self, *index):
        if self.out is None:
            return
        view = (lambda r: r.at[index]) if index else (lambda r: r)
        copy = pltpu.make_async_copy(view(self.ref), view(self.out), self.sems.at[len(self.copies)])
        copy.start()
        self.copies.append(copy)


def project(basis, fields):
    parts = []
    for i, v in enumerate(fields):
        parts.append(lanes_join(nt(basis[i, 0], v), nt(basis[i, 1], v)))
    return jnp.concatenate(parts, axis=0)


def expand(coeff_t, basis, i):
    rank = basis.shape[2]
    c = coeff_t[i * rank : (i + 1) * rank]
    return tn(c.astype(BF16), basis[i, 0]) + tn(lanes_turn(c).astype(BF16), basis[i, 1])


def first_kernel(e_ref, k_ref, s_ref, t_ref, c_ref, pr_ref, fl_ref, nb_ref, out, kept, left, right):
    tc, tiles = pr_ref.ref.shape
    rank, tile = s_ref.ref.shape[2:]
    lanes = tc * rank
    n = out.ref.shape[0]
    width = out.ref.shape[2]
    rows = 2 * e_ref.ref.shape[1]
    columns = tiles * rank
    source = lax.broadcasted_iota(jnp.int32, (tiles, columns), 1) - rank * lax.broadcasted_iota(
        jnp.int32, (tiles, columns), 0
    )
    spread = jnp.where((source >= 0) & (source < rank), 1.0, 0.0).astype(F32)
    lane = lax.broadcasted_iota(jnp.int32, (rank, columns), 1).astype(F32)
    level = lane - rank * jnp.floor((lane + 0.5) / rank)
    top = jnp.maximum(level, lax.broadcasted_iota(jnp.int32, (rank, columns), 0).astype(F32))
    j = lax.broadcasted_iota(jnp.int32, (tc, tiles), 1)
    i = lax.broadcasted_iota(jnp.int32, (tc, tiles), 0) + lax.axis_index("tile") * tc
    distance = i - j
    distance = jnp.where(distance < 0, distance + tiles, distance)
    far = (fl_ref[...] == 1) & (distance != 0) & (distance != 1) & (distance != tiles - 1)
    limit = jnp.where(far, pr_ref[...], 0).astype(F32)
    wide = nn(limit, spread)
    mask = jnp.concatenate([jnp.where(top < wide[a : a + 1], 1.0, 0.0) for a in range(tc)], axis=0)
    m_re = (c_ref[0].astype(F32) * mask).astype(BF16)
    m_im = (c_ref[1].astype(F32) * mask).astype(BF16)
    kept.ref[0] = m_re
    kept.ref[1] = m_im
    kept.send()
    e = stacked(e_ref[...])
    coeff = project(s_ref.get(), [e[:, i * tile : (i + 1) * tile] for i in range(tc)]).astype(BF16)
    k = stacked(k_ref[...])
    proj = project(t_ref.get(), [k[:, i * tile : (i + 1) * tile] for i in range(tc)])
    back = tn(m_re, proj.astype(BF16)) + tn(m_im, lanes_turn(proj).astype(BF16))
    for d in range(n):
        out.ref[d, :, 0:rows] = coeff
        out.ref[d, :, rows:width] = back[d * lanes : (d + 1) * lanes].astype(BF16)
    out.send()
    left.ref[...] = moved(k, nb_ref, tile, 0, 0).astype(BF16)
    left.send()
    right.ref[...] = moved(k, nb_ref, tile, tc - 1, 2).astype(BF16)
    right.send()


def moved(k, nb_ref, tile, i, o):
    own = k[:, i * tile : (i + 1) * tile]
    return rows_join(nt(own, nb_ref[i, o, 0]), nt(own, nb_ref[i, o, 1]))


def near_of(fields, nb_ref, i, offsets):
    p = q = None
    for o in offsets:
        pp, qq = nn(fields[i + o - 1], nb_ref[i, o, 0]), nn(fields[i + o - 1], nb_ref[i, o, 1])
        p, q = (pp, qq) if p is None else (p + pp, q + qq)
    return rows_join(p, q)


def inside_kernel(v_ref, k_ref, nb_ref, near, loc, *, tile, tc):
    v, k = v_ref[...], stacked(k_ref[...])
    fields = {i: v[:, i * tile : (i + 1) * tile] for i in range(tc)}
    for m in range(tc):
        cut = slice(m * tile, (m + 1) * tile)
        near.ref[:, cut] = near_of(fields, nb_ref, m, [o for o in range(3) if m + o - 1 in fields])
        total = None
        for o in range(3):
            i = m + 1 - o
            if 0 <= i < tc:
                part = moved(k, nb_ref, tile, i, o)
                total = part if total is None else total + part
        loc.ref[:, cut] = total


def second_near_kernel(*refs, tile, tc):
    fields = {i: refs[i][...] for i in range(tc)}
    hl_ref, hr_ref, nb_ref, base_ref, out = refs[tc:]
    fields[-1], fields[tc] = hl_ref[...], hr_ref[...]
    for i in range(tc):
        cut = slice(i * tile, (i + 1) * tile)
        out.ref[:, cut] = base_ref[:, cut] - DAMPING * near_of(fields, nb_ref, i, range(3))


def coupled_of(gathered, m_ref):
    turned = lanes_turn(gathered)
    coupled = nn(m_ref[0], gathered) + nn(m_ref[1], turned)
    return coupled.astype(BF16).astype(F32)


def update_kernel(got_ref, m_ref, near_ref, hl_ref, hr_ref, t_ref, e_ref, nb_ref, base, *tiles_out, tile, tc):
    n, lanes, _ = got_ref.ref.shape
    rows = base.ref.shape[0]
    coupled = coupled_of(got_ref[:, :, 0:rows].reshape(n * lanes, rows), m_ref)
    edges = {-1: hl_ref[...], tc: hr_ref[...]}
    for i in range(tc):
        cut = slice(i * tile, (i + 1) * tile)
        total = near_ref[:, cut] + expand(coupled, t_ref.get(), i)
        for o in range(3):
            if i + o - 1 in edges:
                total = total + near_of(edges, nb_ref, i, [o])
        start = stacked(e_ref[:, :, cut]).astype(F32)
        field = start - DAMPING * total
        tiles_out[i].ref[...] = field.astype(BF16)
        base.ref[:, cut] = (1.0 - DAMPING) * field + DAMPING * start
        base.send(slice(None), cut)


def focal_kernel(*refs, tile, tc):
    got_ref, loc_ref, gl_ref, gr_ref = refs[:4]
    fields = [ref[...] for ref in refs[4 : 4 + tc]]
    s_ref, k_ref, e_ref, out, side = refs[4 + tc :]
    n, _, rows = out.ref.shape
    focal = gl_ref.ref.shape[0] // 2
    back = jnp.sum(got_ref[:, :, rows:].astype(F32), axis=0).astype(BF16).astype(F32)
    k = stacked(k_ref[...])
    p = None
    for i in range(tc):
        cut = slice(i * tile, (i + 1) * tile)
        total = loc_ref[:, cut] + expand(back, s_ref.get(), i)
        if i == 0:
            total = total + gl_ref[...].astype(F32)
        if i == tc - 1:
            total = total + gr_ref[...].astype(F32)
        own = (-DAMPING * total).astype(BF16)
        side.ref[:, cut] = own
        start = stacked(e_ref[:, :, cut]).astype(F32)
        mix = ((1.0 - DAMPING) * fields[i].astype(F32) + DAMPING * start).astype(BF16)
        term = nt(k[:, cut], mix) + nt(own, fields[i])
        p = term if p is None else p + term
    half = rows // 2
    part = jnp.concatenate(
        [p[:focal, :half] - p[focal:, half:], p[:focal, half:] + p[focal:, :half]], axis=1
    ).astype(BF16)
    coeff = project(s_ref.get(), fields).astype(BF16)
    for d in range(n):
        out.ref[d, :focal] = part
        out.ref[d, focal:] = coeff


def eye(n):
    return lax.broadcasted_iota(jnp.int32, (n, n), 0) == lax.broadcasted_iota(jnp.int32, (n, n), 1)


def sum_kernel(got_ref, foc, power):
    focal = foc.ref.shape[0]
    half = foc.ref.shape[1] // 2
    total = jnp.sum(got_ref[:, 0:focal].astype(F32), axis=0)
    foc.ref[...] = total
    squares = total[:, :half] * total[:, :half] + total[:, half:] * total[:, half:]
    column = jnp.sum(squares, axis=1, keepdims=True)
    power.ref[...] = jnp.sum(jnp.where(eye(focal), column, 0.0), axis=0, keepdims=True)
    power.send()
    foc.send()


def last_kernel(a_ref, b_ref, c_ref, d_ref, foc_ref, side_ref, target_ref, owner_ref, k_ref, adj, res, *, sources, scale):
    focal = foc_ref.ref.shape[0]
    half = foc_ref.ref.shape[1] // 2
    intensity = (a_ref[...] + b_ref[...]) + (c_ref[...] + d_ref[...])
    row = jnp.tanh(intensity / (2.0 * sources)) - target_ref[...]
    diagonal = eye(focal)
    column = jnp.sum(jnp.where(diagonal, row, 0.0), axis=1, keepdims=True)
    owner = jnp.sum(jnp.where(diagonal, owner_ref[...], 0), axis=1, keepdims=True)
    slots = res.ref.shape[1]
    slot = lax.broadcasted_iota(jnp.int32, (focal, slots), 1) + lax.axis_index("tile") * slots
    res.ref[...] = jnp.sum(jnp.where(owner == slot, column, 0.0), axis=0, keepdims=True)
    res.send()
    re = column * foc_ref[:, :half]
    im = -column * foc_ref[:, half:]
    w = jnp.concatenate([re, im], axis=1).astype(BF16)
    turned = jnp.concatenate([-im, re], axis=1).astype(BF16)
    both = jnp.concatenate([w, turned], axis=0)
    k = stacked(k_ref[...])
    width = k.shape[1]
    tile = width // 2
    for at in range(0, width, tile):
        cut = slice(at, at + tile)
        out = scale * (tn(both, k[:, cut]) + tn(both, side_ref[:, cut]))
        adj.ref[0, :, cut] = out[:half]
        adj.ref[1, :, cut] = out[half:]
        adj.send(slice(None), slice(None), cut)


def field_kernel(got_ref, m_ref, near_ref, t_ref, out, *, tile, tc):
    n, _, rows = got_ref.ref.shape
    lanes = m_ref.ref.shape[1]
    half = rows // 2
    coupled = coupled_of(got_ref[:, -lanes:].reshape(n * lanes, rows), m_ref)
    for i in range(tc):
        cut = slice(i * tile, (i + 1) * tile)
        field = near_ref[:, cut] - DAMPING * expand(coupled, t_ref.get(), i)
        out.ref[0, :, cut] = field[:half]
        out.ref[1, :, cut] = field[half:]
        out.send(slice(None), slice(None), cut)


def edges_kernel(v_ref, left_ref, right_ref, sems):
    width, tile = v_ref.shape[1], left_ref.shape[1]
    copies = [
        pltpu.make_async_copy(v_ref.at[:, 0:tile], left_ref, sems.at[0]),
        pltpu.make_async_copy(v_ref.at[:, width - tile : width], right_ref, sems.at[1]),
    ]
    for copy in copies:
        copy.start()
    for copy in copies:
        copy.wait()


VM = pl.BlockSpec(memory_space=pltpu.VMEM)
FAR = pl.BlockSpec(memory_space=pltpu.HBM)


def in_hbm(x):
    return pltpu.with_memory_space_constraint(x, pltpu.HBM)


def padded(one):
    return math.prod(one.shape[:-1]) * -(-one.shape[-1] // 128) * 128 * jnp.dtype(one.dtype).itemsize


def call(kernel, outs, near, far=(), blocks=(), far_outs=()):
    far = [in_hbm(arg) for arg in far]
    held = [len(blocks) if arg.ndim == 5 and blocks else 0 for arg in far]
    scratch = [
        pltpu.VMEM((count,) + arg.shape[2:] if count else arg.shape, arg.dtype) for arg, count in zip(far, held)
    ]
    scratch += [pltpu.VMEM(*outs[o]) for o in far_outs]
    taken = sum(padded(one) for one in scratch) + 3 * sum(padded(jax.ShapeDtypeStruct(s, d)) for s, d in outs)
    taken += 2 * sum(padded(one) for one in near)
    scratch += [pltpu.SemaphoreType.DMA((sum(count or 1 for count in held) + 1,))]
    scratch += [pltpu.SemaphoreType.DMA((len(far_outs) + 1, 8))]

    def run(*refs):
        refs = list(refs)
        close = [Operand(None, refs.pop(0)) for _ in near]
        sources = [refs.pop(0) for _ in far]
        sinks = [refs.pop(0) for _ in outs]
        places = [refs.pop(0) for _ in far]
        stages = {o: refs.pop(0) for o in far_outs}
        ins, ends = refs
        operands, at = [], 0
        for source, place, count in zip(sources, places, held):
            if count:
                parts = {}
                for spot, block in enumerate(blocks):
                    copy = pltpu.make_async_copy(source.at[block], place.at[spot], ins.at[at])
                    copy.start()
                    at += 1
                    parts[block] = Operand(copy, place.at[spot])
                operands.append(Blocks(parts))
            else:
                copy = pltpu.make_async_copy(source, place, ins.at[at])
                copy.start()
                at += 1
                operands.append(Operand(copy, place))
        results = []
        for o, sink in enumerate(sinks):
            results.append(Result(stages[o], sink, ends.at[far_outs.index(o)]) if o in stages else Result(sink))
        kernel(*close, *operands, *results)
        for operand in operands:
            for one in operand.operands.values() if isinstance(operand, Blocks) else [operand]:
                one.get()
        for result in results:
            for copy in result.copies:
                copy.wait()

    return pl.pallas_call(
        run,
        out_shape=[jax.ShapeDtypeStruct(s, d) for s, d in outs],
        in_specs=[VM] * len(near) + [FAR] * len(far),
        out_specs=[FAR if o in far_outs else VM for o in range(len(outs))],
        scratch_shapes=scratch,
        compiler_params=pltpu.CompilerParams(vmem_limit_bytes=min(taken + (12 << 20), 60 * 1024 * 1024)),
    )(*near, *far)


def per_device(e, nb, sb, tb, coupling, pair_rank, far_link, fk, target, owner):
    tc, _, _, tile, _ = nb.shape
    rank = sb.shape[2]
    lanes = tc * rank
    half = e.shape[1]
    rows = 2 * half
    width = e.shape[2]
    tiles = pair_rank.shape[0]
    focal = target.shape[0]
    n = lax.axis_size("tile")
    groups = lax.axis_size("src")
    slots = focal // n
    edges = [(0, 0), (tc - 1, 2)]
    inside = [(i, o) for i in range(tc) for o in range(3) if (i, o) not in edges]
    sizes = dict(tile=tile, tc=tc)
    up = [(i, (i + 1) % n) for i in range(n)]
    down = [(j, i) for i, j in up]

    def exchange(to_left, to_right):
        return lax.ppermute(to_right, "tile", up), lax.ppermute(to_left, "tile", down)

    flat = stacked(e)
    every = [(i, o) for i in range(tc) for o in range(3)]
    el, er = pl.pallas_call(
        edges_kernel,
        out_shape=[jax.ShapeDtypeStruct((rows, tile), BF16)] * 2,
        in_specs=[FAR],
        out_specs=[VM, VM],
        scratch_shapes=[pltpu.SemaphoreType.DMA((2,))],
        compiler_params=pltpu.CompilerParams(vmem_limit_bytes=8 << 20),
        name="ends",
    )(in_hbm(flat))
    hl, hr = exchange(el, er)
    send, masked, gl, gr = call(
        first_kernel,
        [
            ((n, lanes, rows + 2 * focal), BF16),
            ((2, lanes, tiles * rank), BF16),
            ((2 * focal, tile), BF16),
            ((2 * focal, tile), BF16),
        ],
        [], [e, fk, sb, tb, jnp.swapaxes(coupling, 1, 2), pair_rank.T, far_link.T, nb], blocks=edges,
    )
    got = lax.all_to_all(send, "tile", split_axis=0, concat_axis=0, tiled=True)
    from_left, from_right = exchange(gl, gr)
    near, loc = call(
        functools.partial(inside_kernel, **sizes),
        [((rows, width), F32), ((2 * focal, width), F32)],
        [], [flat, fk, nb], blocks=inside,
    )
    base, *f1 = call(
        functools.partial(update_kernel, **sizes),
        [((rows, width), F32)] + [((rows, tile), BF16)] * tc,
        [got, masked, near, hl, hr], [tb, e, nb], blocks=edges, far_outs=(0,),
    )
    hl1, hr1 = exchange(f1[0], f1[-1])
    send1, side = call(
        functools.partial(focal_kernel, **sizes),
        [((n, focal + lanes, rows), BF16), ((2 * focal, width), BF16)],
        [got, loc, from_left, from_right, *f1], [sb, fk, e],
    )
    got1 = lax.all_to_all(send1, "tile", split_axis=0, concat_axis=0, tiled=True)
    (near1,) = call(
        functools.partial(second_near_kernel, **sizes), [((rows, width), F32)],
        [*f1, hl1, hr1], [nb, base], blocks=every,
    )
    foc, part = call(sum_kernel, [((focal, rows), F32), ((1, focal), F32)], [got1])
    parts = [part] + [lax.ppermute(part, "src", [(i, i ^ k) for i in range(groups)]) for k in (1, 2, 3)]
    adjoint, residual = call(
        functools.partial(last_kernel, sources=half * groups, scale=(tiles * tile / focal) ** 0.5),
        [((2, half, width), F32), ((1, slots), F32)],
        [*parts, foc, side], [target[None], owner[None], fk], far_outs=(0, 1),
    )
    (field,) = call(
        functools.partial(field_kernel, **sizes), [((2, half, width), F32)],
        [got1, masked, near1], [tb], far_outs=(0,),
    )
    return field, residual[0], adjoint


def solution(mesh):
    return jax.shard_map(
        per_device,
        mesh=mesh,
        in_specs=(
            P(None, "src", "tile"),
            P("tile", None, None, None, None),
            P("tile", None, None, None),
            P("tile", None, None, None),
            P(None, None, "tile"),
            P(None, "tile"),
            P(None, "tile"),
            P(None, None, "tile"),
            P(),
            P(),
        ),
        out_specs=(P(None, "src", "tile"), P("tile"), P(None, "src", "tile")),
        check_vma=False,
    )
```

```python
import functools
import math

import jax
import jax.numpy as jnp
from jax import lax
from jax.experimental import pallas as pl
from jax.experimental.pallas import tpu as pltpu
from jax.sharding import PartitionSpec as P


DAMPING = 0.8
IN_FLIGHT = 16 << 20
F32 = jnp.float32
BF16 = jnp.bfloat16


def nn(a, b):
    return lax.dot_general(a, b, (((1,), (0,)), ((), ())), preferred_element_type=F32)


def nt(a, b):
    return lax.dot_general(a, b, (((1,), (1,)), ((), ())), preferred_element_type=F32)


def tn(a, b):
    return lax.dot_general(a, b, (((0,), (0,)), ((), ())), preferred_element_type=F32)


def rows_join(p, q):
    h = p.shape[0] // 2
    return jnp.concatenate([p[:h] - q[h:], p[h:] + q[:h]], axis=0)


def lanes_join(p, q):
    h = p.shape[1] // 2
    return jnp.concatenate([p[:, :h] - q[:, h:], p[:, h:] + q[:, :h]], axis=1)


def lanes_turn(x):
    h = x.shape[1] // 2
    return jnp.concatenate([-x[:, h:], x[:, :h]], axis=1)


def is_even():
    return lax.rem(lax.axis_index("tile"), 2) == 0


def put(near, far, left, right):
    @pl.when(is_even())
    def _():
        near[...], far[...] = right, left

    @pl.when(jnp.logical_not(is_even()))
    def _():
        near[...], far[...] = left, right


def sides(near, far):
    even = is_even()
    return jnp.where(even, far, near), jnp.where(even, near, far)


def stacked(x):
    return x.reshape(x.shape[0] * x.shape[1], x.shape[2])


class Queue:
    def __init__(self):
        self.waiting, self.flying = [], 0

    def add(self, copy, size):
        self.waiting.append((copy, size))

    def pump(self):
        while self.waiting and self.flying < IN_FLIGHT:
            copy, size = self.waiting.pop(0)
            copy.start()
            self.flying += size


class Operand:
    def __init__(self, ref, copy=None, queue=None):
        self.ref, self.copy, self.queue = ref, copy, queue
        if copy is not None:
            queue.add(copy, padded(ref))

    def get(self):
        if self.copy is not None:
            while any(copy is self.copy for copy, _ in self.queue.waiting):
                self.queue.flying = 0
                self.queue.pump()
            self.copy.wait()
            self.copy = None
            self.queue.flying -= padded(self.ref)
            self.queue.pump()
        return self.ref

    def __getitem__(self, index):
        return self.get()[index]


class Blocks:
    def __init__(self, operands):
        self.operands = operands

    def __getitem__(self, index):
        return self.operands[index[:2]][index[2:] + (slice(None),) * (3 - len(index[2:]))]


class Result:
    def __init__(self, ref, out=None, sems=None):
        self.ref, self.out, self.sems, self.copies = ref, out, sems, []

    def send(self, *index):
        if self.out is None:
            return
        view = (lambda r: r.at[index]) if index else (lambda r: r)
        copy = pltpu.make_async_copy(view(self.ref), view(self.out), self.sems.at[len(self.copies)])
        copy.start()
        self.copies.append(copy)


def project(basis, fields):
    parts = []
    for i, v in enumerate(fields):
        parts.append(lanes_join(nt(basis[i, 0], v), nt(basis[i, 1], v)))
    return jnp.concatenate(parts, axis=0)


def far_of(c, basis_re, basis_im):
    return tn(c.astype(BF16), basis_re) + tn(lanes_turn(c).astype(BF16), basis_im)


def expand(coeff_t, basis, i):
    rank = basis.shape[2]
    return far_of(coeff_t[i * rank : (i + 1) * rank], basis[i, 0], basis[i, 1])


def first_kernel(e_ref, k_ref, s_ref, t_ref, c_ref, pr_ref, fl_ref, nb_ref, out, kept, left, right):
    tc, tiles = pr_ref.ref.shape
    rank, tile = s_ref.ref.shape[2:]
    lanes = tc * rank
    n = out.ref.shape[0]
    width = out.ref.shape[2]
    rows = 2 * e_ref.ref.shape[1]
    columns = tiles * rank
    source = lax.broadcasted_iota(jnp.int32, (tiles, columns), 1) - rank * lax.broadcasted_iota(
        jnp.int32, (tiles, columns), 0
    )
    spread = jnp.where((source >= 0) & (source < rank), 1.0, 0.0).astype(F32)
    lane = lax.broadcasted_iota(jnp.int32, (rank, columns), 1).astype(F32)
    level = lane - rank * jnp.floor((lane + 0.5) / rank)
    top = jnp.maximum(level, lax.broadcasted_iota(jnp.int32, (rank, columns), 0).astype(F32))
    j = lax.broadcasted_iota(jnp.int32, (tc, tiles), 1)
    i = lax.broadcasted_iota(jnp.int32, (tc, tiles), 0) + lax.axis_index("tile") * tc
    distance = i - j
    distance = jnp.where(distance < 0, distance + tiles, distance)
    far = (fl_ref[...] == 1) & (distance != 0) & (distance != 1) & (distance != tiles - 1)
    limit = jnp.where(far, pr_ref[...], 0).astype(F32)
    wide = nn(limit, spread)
    mask = jnp.concatenate([jnp.where(top < wide[a : a + 1], 1.0, 0.0) for a in range(tc)], axis=0)
    m_re = (c_ref[0].astype(F32) * mask).astype(BF16)
    m_im = (c_ref[1].astype(F32) * mask).astype(BF16)
    kept.ref[0] = m_re
    kept.ref[1] = m_im
    kept.send()
    e = stacked(e_ref[...])
    coeff = project(s_ref.get(), [e[:, i * tile : (i + 1) * tile] for i in range(tc)]).astype(BF16)
    k = stacked(k_ref[...])
    proj = project(t_ref.get(), [k[:, i * tile : (i + 1) * tile] for i in range(tc)])
    back = tn(m_re, proj.astype(BF16)) + tn(m_im, lanes_turn(proj).astype(BF16))
    for d in range(n):
        out.ref[d, :, 0:rows] = coeff
        out.ref[d, :, rows:width] = back[d * lanes : (d + 1) * lanes].astype(BF16)
    out.send()
    pair = lax.rem(lax.axis_index("src"), 2)
    part = k_ref.ref.shape[1] // 2
    own = stacked(k_ref.get()[:, pl.ds(pl.multiple_of(pair * part, part), part), :])
    sent = []
    for i, o in ((0, 0), (tc - 1, 2)):
        share = moved(own, nb_ref, tile, i, o).astype(BF16)
        rows_of = [t_ref[i, 0].astype(F32), t_ref[i, 1].astype(F32)]
        for at in range(0, columns, tile):
            end = min(columns, at + tile)
            for m in (m_re, m_im):
                piece = m[:, at:end].astype(F32)[i * rank : (i + 1) * rank]
                if end - at < tile:
                    piece = jnp.concatenate([piece, jnp.zeros((rank, tile - end + at), F32)], axis=1)
                rows_of.append(piece)
        factors = jnp.concatenate(rows_of, axis=0)
        half = factors.shape[0] // 2
        factors = jnp.where(pair == 0, factors[:half], factors[half:]).astype(BF16)
        sent.append(jnp.concatenate([share, factors], axis=0))
    put(left.ref, right.ref, *sent)


def moved(k, nb_ref, tile, i, o):
    own = k[:, i * tile : (i + 1) * tile]
    return rows_join(nt(own, nb_ref[i, o, 0]), nt(own, nb_ref[i, o, 1]))


def near_of(fields, nb_ref, i, offsets):
    p = q = None
    for o in offsets:
        pp, qq = nn(fields[i + o - 1], nb_ref[i, o, 0]), nn(fields[i + o - 1], nb_ref[i, o, 1])
        p, q = (pp, qq) if p is None else (p + pp, q + qq)
    return rows_join(p, q)


def inside_kernel(v_ref, k_ref, nb_ref, loc, near, early, *, tile, tc):
    v, k = v_ref[...], stacked(k_ref[...])
    fields = {i: v[:, i * tile : (i + 1) * tile] for i in range(tc)}
    for m in range(tc):
        near.ref[:, m * tile : (m + 1) * tile] = near_of(fields, nb_ref, m, [o for o in range(3) if m + o - 1 in fields])
        total = None
        for o in range(3):
            if 0 <= m + 1 - o < tc:
                part = moved(k, nb_ref, tile, m + 1 - o, o)
                total = part if total is None else total + part
        cut = slice(m * tile, (m + 1) * tile)
        loc.ref[:, cut] = total
        loc.send(slice(None), cut)
    early.ref[...] = DAMPING * nt(k, v)


def edge_kernel(near_ref, hl_ref, hr_ref, v_ref, nb_ref, start, left, right, *, tile, tc):
    fields = dict(zip((-1, tc), sides(hl_ref[...], hr_ref[...])))
    v = v_ref[...]
    ends = {}
    for i in range(tc):
        cut = slice(i * tile, (i + 1) * tile)
        near = near_ref[:, cut]
        for o in range(3):
            if i + o - 1 in fields:
                near = near + near_of(fields, nb_ref, i, [o])
        value = v[:, cut].astype(F32) - DAMPING * near
        start.ref[:, cut] = value
        ends[i] = value.astype(BF16)
    put(left.ref, right.ref, ends[0], ends[tc - 1])


def second_near_kernel(*refs, tile, tc):
    fields = {i: refs[i][...] for i in range(tc)}
    hl_ref, hr_ref, edge_ref, bases_ref, e_ref, nb_ref, out = refs[tc:]
    for at, (i, h) in enumerate(zip((-1, tc), sides(hl_ref[...], hr_ref[...]))):
        far = far_of(edge_ref[at], bases_ref[at, 0], bases_ref[at, 1])
        fields[i] = (h.astype(F32) - DAMPING * far).astype(BF16)
    for i in range(tc):
        cut = slice(i * tile, (i + 1) * tile)
        near = near_of(fields, nb_ref, i, range(3))
        start = (1.0 - DAMPING) * fields[i].astype(F32) + DAMPING * stacked(e_ref[:, :, cut]).astype(F32)
        out.ref[:, cut] = start - DAMPING * near


def coupled_of(gathered, m_ref):
    turned = lanes_turn(gathered)
    coupled = nn(m_ref[0], gathered) + nn(m_ref[1], turned)
    return coupled.astype(BF16).astype(F32)


def middle_kernel(*refs, tile, tc):
    got_ref, m_ref, t_ref, start_ref, s_ref, gl_ref, ol_ref, gr_ref, or_ref, early_ref, loc_ref, k_ref = refs[:12]
    tiles_out, (side, out, edge, bases) = refs[12 : 12 + tc], refs[12 + tc :]
    n, lanes, _ = got_ref.ref.shape
    rows = out.ref.shape[1]
    focal = k_ref.ref.shape[1]
    rank = t_ref.ref.shape[2]
    columns = n * lanes
    first = lax.rem(lax.axis_index("src"), 2) == 0

    def whole(own, other):
        own, other = own.astype(F32), other.astype(F32)
        low, high = jnp.where(first, own, other), jnp.where(first, other, own)
        half = focal // 2
        share = jnp.concatenate([low[:half], high[:half], low[half:focal], high[half:focal]], axis=0)
        factors = jnp.concatenate([low[focal:], high[focal:]], axis=0)
        basis = [factors[p * rank : (p + 1) * rank].astype(BF16) for p in range(2)]
        turns = []
        for p in range(2):
            pieces = [
                factors[(2 + 2 * c + p) * rank : (3 + 2 * c + p) * rank] for c in range(-(-columns // tile))
            ]
            turns.append((jnp.concatenate(pieces, axis=1) if len(pieces) > 1 else pieces[0])[:, :columns])
        return share, basis, turns

    (gl, gr), (ol, on_right) = sides(gl_ref[...], gr_ref[...]), sides(ol_ref[...], or_ref[...])
    share_l, basis_l, turns_l = whole(gl, ol)
    share_r, basis_r, turns_r = whole(gr, on_right)

    gathered = got_ref[:, :, 0:rows].reshape(columns, rows)
    stack = [
        jnp.concatenate([turns_l[p], m_ref[p].astype(F32), turns_r[p]], axis=0).astype(BF16) for p in range(2)
    ]
    coupled = (nn(stack[0], gathered) + nn(stack[1], lanes_turn(gathered))).astype(BF16).astype(F32)
    fields = []
    for i in range(tc):
        far = far_of(coupled[(i + 1) * rank : (i + 2) * rank], t_ref[i, 0], t_ref[i, 1])
        field = start_ref[:, i * tile : (i + 1) * tile] - DAMPING * far
        fields.append(field.astype(BF16))
        tiles_out[i].ref[...] = fields[i]
    edge.ref[0], edge.ref[1] = coupled[:rank], coupled[(tc + 1) * rank :]
    for p in range(2):
        bases.ref[0, p], bases.ref[1, p] = basis_l[p], basis_r[p]
    back = jnp.sum(got_ref[:, :, rows:].astype(F32), axis=0).astype(BF16).astype(F32)
    k = stacked(k_ref[...])
    p = early_ref[...]
    half = rows // 2
    for i in range(tc):
        cut = slice(i * tile, (i + 1) * tile)
        total = loc_ref[:, cut] + expand(back, s_ref.get(), i)
        if i == 0:
            total = total + share_l
        if i == tc - 1:
            total = total + share_r
        own = (-DAMPING * total).astype(BF16)
        side.ref[:, cut] = own
        side.send(slice(None), cut)
        p = p + (1.0 - DAMPING) * nt(k[:, cut], fields[i]) + nt(own, fields[i])
    half = rows // 2
    part = jnp.concatenate(
        [p[:focal, :half] - p[focal:, half:], p[:focal, half:] + p[focal:, :half]], axis=1
    ).astype(BF16)
    coeff = project(s_ref.get(), fields).astype(BF16)
    out.ref[:focal] = part
    out.ref[focal:] = coeff


def eye(n):
    return lax.broadcasted_iota(jnp.int32, (n, n), 0) == lax.broadcasted_iota(jnp.int32, (n, n), 1)


def pair_kernel(own_ref, other_ref, out, *, focal, group):
    lanes = own_ref.ref.shape[0] - focal
    first = lax.rem(lax.axis_index("tile") // group, 2) == 0
    own, other = own_ref[...].astype(F32), other_ref[...].astype(F32)
    out.ref[:focal] = (own[:focal] + other[:focal]).astype(BF16)
    out.ref[focal : focal + lanes] = jnp.where(first, own[focal:], other[focal:]).astype(BF16)
    out.ref[focal + lanes :] = jnp.where(first, other[focal:], own[focal:]).astype(BF16)


def sum_kernel(*refs, focal):
    gots, (foc, power) = refs[:-2], refs[-2:]
    half = foc.ref.shape[1] // 2
    total = gots[0][:focal].astype(F32)
    for got in gots[1:]:
        total = total + got[:focal].astype(F32)
    foc.ref[...] = total
    squares = total[:, :half] * total[:, :half] + total[:, half:] * total[:, half:]
    column = jnp.sum(squares, axis=1, keepdims=True)
    power.ref[...] = jnp.sum(jnp.where(eye(focal), column, 0.0), axis=0, keepdims=True)


def last_kernel(a_ref, b_ref, c_ref, d_ref, foc_ref, target_ref, owner_ref, k_ref, side_ref, adj, res, *, sources, scale):
    focal = foc_ref.ref.shape[0]
    half = foc_ref.ref.shape[1] // 2
    intensity = (a_ref[...] + b_ref[...]) + (c_ref[...] + d_ref[...])
    row = jnp.tanh(intensity / (2.0 * sources)) - target_ref[...]
    diagonal = eye(focal)
    column = jnp.sum(jnp.where(diagonal, row, 0.0), axis=1, keepdims=True)
    owner = jnp.sum(jnp.where(diagonal, owner_ref[...], 0), axis=1, keepdims=True)
    slots = res.ref.shape[1]
    slot = lax.broadcasted_iota(jnp.int32, (focal, slots), 1) + lax.axis_index("tile") * slots
    res.ref[...] = jnp.sum(jnp.where(owner == slot, column, 0.0), axis=0, keepdims=True)
    res.send()
    re = column * foc_ref[:, :half]
    im = -column * foc_ref[:, half:]
    w = jnp.concatenate([re, im], axis=1).astype(BF16)
    turned = jnp.concatenate([-im, re], axis=1).astype(BF16)
    both = jnp.concatenate([w, turned], axis=0)
    k = stacked(k_ref[...])
    width = k.shape[1]
    tile = width // 2
    for at in range(0, width, tile):
        cut = slice(at, at + tile)
        out = scale * (tn(both, k[:, cut]) + tn(both, side_ref[:, cut]))
        adj.ref[0, :, cut] = out[:half]
        adj.ref[1, :, cut] = out[half:]
        adj.send(slice(None), slice(None), cut)


def field_kernel(*refs, tile, tc, focal, group):
    gots, (m_ref, near_ref, t_ref, out) = refs[:-5], refs[-5:-1]
    all_ref = refs[-1]
    rows = all_ref.shape[1]
    half = rows // 2
    pair = gots[0].ref.shape[0] - focal
    here = lax.axis_index("tile") // group
    for k, got in enumerate(gots):
        at = jnp.bitwise_xor(here, k)
        all_ref[pl.ds(pl.multiple_of(at * pair, pair), pair), :] = got[focal:]
    coupled = coupled_of(all_ref[...], m_ref)
    for i in range(tc):
        cut = slice(i * tile, (i + 1) * tile)
        field = near_ref[:, cut] - DAMPING * expand(coupled, t_ref.get(), i)
        out.ref[0, :, cut] = field[:half]
        out.ref[1, :, cut] = field[half:]
        out.send(slice(None), slice(None), cut)


def edges_kernel(v_ref, near_ref, far_ref, sems):
    width, tile = v_ref.shape[1], near_ref.shape[1]
    odd = lax.rem(lax.axis_index("tile"), 2)
    copies = []
    for at, (ref, side) in enumerate(((near_ref, 1 - odd), (far_ref, odd))):
        begin = pl.multiple_of(side * (width - tile), 128)
        copies.append(pltpu.make_async_copy(v_ref.at[:, pl.ds(begin, tile)], ref, sems.at[at]))
    for copy in copies:
        copy.start()
    for copy in copies:
        copy.wait()


VM = pl.BlockSpec(memory_space=pltpu.VMEM)
FAR = pl.BlockSpec(memory_space=pltpu.HBM)


def in_hbm(x):
    return pltpu.with_memory_space_constraint(x, pltpu.HBM)


def padded(one):
    return math.prod(one.shape[:-1]) * -(-one.shape[-1] // 128) * 128 * jnp.dtype(one.dtype).itemsize


def call(kernel, outs, near, far=(), blocks=(), far_outs=(), extra=()):
    far = [in_hbm(arg) for arg in far]
    held = [len(blocks) if arg.ndim == 5 and blocks else 0 for arg in far]
    scratch = [
        pltpu.VMEM((count,) + arg.shape[2:] if count else arg.shape, arg.dtype) for arg, count in zip(far, held)
    ]
    scratch += [pltpu.VMEM(*outs[o]) for o in far_outs]
    scratch += [pltpu.VMEM(*one) for one in extra]
    taken = sum(padded(one) for one in scratch) + 3 * sum(padded(jax.ShapeDtypeStruct(s, d)) for s, d in outs)
    taken += 2 * sum(padded(one) for one in near)
    scratch += [pltpu.SemaphoreType.DMA((sum(count or 1 for count in held) + 1,))]
    scratch += [pltpu.SemaphoreType.DMA((len(far_outs) + 1, 8))]

    def run(*refs):
        refs = list(refs)
        close = [Operand(refs.pop(0)) for _ in near]
        queue = Queue()
        sources = [refs.pop(0) for _ in far]
        sinks = [refs.pop(0) for _ in outs]
        places = [refs.pop(0) for _ in far]
        stages = {o: refs.pop(0) for o in far_outs}
        more, (ins, ends) = refs[: len(extra)], refs[len(extra) :]
        operands, at = [], 0
        for source, place, count in zip(sources, places, held):
            if count:
                parts = {}
                for spot, block in enumerate(blocks):
                    copy = pltpu.make_async_copy(source.at[block], place.at[spot], ins.at[at])
                    at += 1
                    parts[block] = Operand(place.at[spot], copy, queue)
                operands.append(Blocks(parts))
            else:
                operands.append(Operand(place, pltpu.make_async_copy(source, place, ins.at[at]), queue))
                at += 1
        queue.pump()
        results = []
        for o, sink in enumerate(sinks):
            results.append(Result(stages[o], sink, ends.at[far_outs.index(o)]) if o in stages else Result(sink))
        kernel(*close, *operands, *results, *more)
        for operand in operands:
            for one in operand.operands.values() if isinstance(operand, Blocks) else [operand]:
                one.get()
        for result in results:
            for copy in result.copies:
                copy.wait()

    return pl.pallas_call(
        run,
        out_shape=[
            pltpu.HBM(s, d) if o in far_outs else jax.ShapeDtypeStruct(s, d) for o, (s, d) in enumerate(outs)
        ],
        in_specs=[VM] * len(near) + [FAR] * len(far),
        out_specs=[FAR if o in far_outs else VM for o in range(len(outs))],
        scratch_shapes=scratch,
        compiler_params=pltpu.CompilerParams(vmem_limit_bytes=min(taken + (12 << 20), 60 * 1024 * 1024)),
    )(*near, *far)


def per_device(e, nb, sb, tb, coupling, pair_rank, far_link, fk, target, owner):
    tc, _, _, tile, _ = nb.shape
    rank = sb.shape[2]
    lanes = tc * rank
    half = e.shape[1]
    rows = 2 * half
    width = e.shape[2]
    tiles = pair_rank.shape[0]
    focal = target.shape[0]
    n = lax.axis_size("tile")
    groups = lax.axis_size("src")
    slots = focal // n
    edges = [(0, 0), (tc - 1, 2)]
    inside = [(i, o) for i in range(tc) for o in range(3) if (i, o) not in edges]
    sizes = dict(tile=tile, tc=tc)
    every = [(i, o) for i in range(tc) for o in range(3)]
    within = [(i, i ^ 1) for i in range(n)]
    across = [(i, (i - 1 + 2 * (i % 2)) % n) for i in range(n)]

    def exchange(near, far):
        return lax.ppermute(near, "tile", within), lax.ppermute(far, "tile", across)

    flat = stacked(e)
    el, er = pl.pallas_call(
        edges_kernel,
        out_shape=[jax.ShapeDtypeStruct((rows, tile), BF16)] * 2,
        in_specs=[FAR],
        out_specs=[VM, VM],
        scratch_shapes=[pltpu.SemaphoreType.DMA((2,))],
        compiler_params=pltpu.CompilerParams(vmem_limit_bytes=8 << 20),
        name="ends",
    )(in_hbm(flat))
    hl, hr = exchange(el, er)
    send, masked, gl, gr = call(
        first_kernel,
        [
            ((n, lanes, rows + 2 * focal), BF16),
            ((2, lanes, tiles * rank), BF16),
            ((focal + rank * (1 + -(-tiles * rank // tile)), tile), BF16),
            ((focal + rank * (1 + -(-tiles * rank // tile)), tile), BF16),
        ],
        [], [e, fk, sb, tb, jnp.swapaxes(coupling, 1, 2), pair_rank.T, far_link.T, nb], blocks=edges,
    )
    got = lax.all_to_all(send, "tile", split_axis=0, concat_axis=0, tiled=True)
    from_left, from_right = exchange(gl, gr)
    loc, near, early = call(
        functools.partial(inside_kernel, **sizes),
        [((2 * focal, width), F32), ((rows, width), F32), ((2 * focal, rows), F32)],
        [], [flat, fk, nb], blocks=inside, far_outs=(0,),
    )
    start, ql, qr = call(
        functools.partial(edge_kernel, **sizes),
        [((rows, width), F32), ((rows, tile), BF16), ((rows, tile), BF16)],
        [near, hl, hr], [flat, nb], blocks=edges,
    )
    hl1, hr1 = exchange(ql, qr)
    swap = [(i, i ^ 1) for i in range(groups)]
    other_left, other_right = lax.ppermute(from_left, "src", swap), lax.ppermute(from_right, "src", swap)
    *f1, side, send1, edge, bases = call(
        functools.partial(middle_kernel, **sizes),
        [((rows, tile), BF16)] * tc
        + [
            ((2 * focal, width), BF16),
            ((focal + lanes, rows), BF16),
            ((2, rank, rows), F32),
            ((2, 2, rank, tile), BF16),
        ],
        [got, masked, tb, start, sb, from_left, other_left, from_right, other_right, early], [loc, fk],
        far_outs=(tc,),
    )
    group = 1
    while n // group > 4:
        other = lax.ppermute(send1, "tile", [(i, i ^ group) for i in range(n)])
        (send1,) = call(
            functools.partial(pair_kernel, focal=focal, group=group),
            [((focal + 2 * group * lanes, rows), BF16)], [send1, other],
        )
        group *= 2
    gots = [send1]
    for k in range(group, n, group):
        gots.append(lax.ppermute(send1, "tile", [(i, i ^ k) for i in range(n)]))
    (near1,) = call(
        functools.partial(second_near_kernel, **sizes), [((rows, width), F32)],
        [*f1, hl1, hr1, edge, bases], [e, nb], blocks=every,
    )
    foc, part = call(functools.partial(sum_kernel, focal=focal), [((focal, rows), F32), ((1, focal), F32)], gots)
    parts = [part] + [lax.ppermute(part, "src", [(i, i ^ k) for i in range(groups)]) for k in (1, 2, 3)]
    adjoint, residual = call(
        functools.partial(last_kernel, sources=half * groups, scale=(tiles * tile / focal) ** 0.5),
        [((2, half, width), F32), ((1, slots), F32)],
        [*parts, foc], [target[None], owner[None], fk, side], far_outs=(0, 1),
    )
    (field,) = call(
        functools.partial(field_kernel, focal=focal, group=group, **sizes), [((2, half, width), F32)],
        [*gots, masked, near1, tb], far_outs=(0,), extra=[((n * lanes, rows), BF16)],
    )
    return field, residual[0], adjoint


def solution(mesh):
    return jax.shard_map(
        per_device,
        mesh=mesh,
        in_specs=(
            P(None, "src", "tile"),
            P("tile", None, None, None, None),
            P("tile", None, None, None),
            P("tile", None, None, None),
            P(None, None, "tile"),
            P(None, "tile"),
            P(None, "tile"),
            P(None, None, "tile"),
            P(),
            P(),
        ),
        out_specs=(P(None, "src", "tile"), P("tile"), P(None, "src", "tile")),
        check_vma=False,
    )
```

```python
import functools
import math

import jax
import jax.numpy as jnp
from jax import lax
from jax.experimental import pallas as pl
from jax.experimental.pallas import tpu as pltpu
from jax.sharding import PartitionSpec as P


DAMPING = 0.8
IN_FLIGHT = 16 << 20
F32 = jnp.float32
BF16 = jnp.bfloat16


def nn(a, b):
    return lax.dot_general(a, b, (((1,), (0,)), ((), ())), preferred_element_type=F32)


def nt(a, b):
    return lax.dot_general(a, b, (((1,), (1,)), ((), ())), preferred_element_type=F32)


def tn(a, b):
    return lax.dot_general(a, b, (((0,), (0,)), ((), ())), preferred_element_type=F32)


def rows_join(p, q):
    h = p.shape[0] // 2
    return jnp.concatenate([p[:h] - q[h:], p[h:] + q[:h]], axis=0)


def lanes_join(p, q):
    h = p.shape[1] // 2
    return jnp.concatenate([p[:, :h] - q[:, h:], p[:, h:] + q[:, :h]], axis=1)


def lanes_turn(x):
    h = x.shape[1] // 2
    return jnp.concatenate([-x[:, h:], x[:, :h]], axis=1)


def is_even():
    return lax.rem(lax.axis_index("tile"), 2) == 0


def put(near, far, left, right):
    @pl.when(is_even())
    def _():
        near[...], far[...] = right, left

    @pl.when(jnp.logical_not(is_even()))
    def _():
        near[...], far[...] = left, right


def sides(near, far):
    even = is_even()
    return jnp.where(even, far, near), jnp.where(even, near, far)


def bit_of(b):
    return lax.rem(lax.axis_index("tile") // b, 2)


def fold_bits(n):
    return [1 << b for b in range(1, n.bit_length() - 2)]


def spread_offsets(n):
    return (1, n // 2, 1 + n // 2)


def dealt(n):
    spread = (0,) + spread_offsets(n)
    order = [0]
    for b in fold_bits(n):
        order = [d + x for d in order for x in (0, b)]
    return [d + x for d in order for x in spread]


def pack(block, rows):
    lanes, width = block.shape
    if width < rows:
        deep = lanes * width // rows
        return jnp.concatenate([block[a : a + deep] for a in range(0, lanes, deep)], axis=1)
    return jnp.concatenate([block[:, a : a + rows] for a in range(0, width, rows)], axis=0)


def unpack(block, lanes):
    deep, rows = block.shape
    if deep < lanes:
        width = deep * rows // lanes
        return jnp.concatenate([block[:, a : a + width] for a in range(0, rows, width)], axis=0)
    return jnp.concatenate([block[a : a + lanes] for a in range(0, deep, lanes)], axis=1)


def place(all_ref, gots, n, lanes, skip=0):
    bits = fold_bits(n)
    for k, got in zip((0,) + spread_offsets(n), gots):
        base = jnp.bitwise_and(jnp.bitwise_xor(lax.axis_index("tile"), k), n - 1 - sum(bits))
        for j in range(1 << len(bits)):
            device = base + sum(b for f, b in enumerate(bits) if (j >> f) & 1)
            at = pl.multiple_of(device * lanes, lanes)
            all_ref[pl.ds(at, lanes), :] = got[skip + j * lanes : skip + (j + 1) * lanes]


def stacked(x):
    return x.reshape(x.shape[0] * x.shape[1], x.shape[2])


class Queue:
    def __init__(self):
        self.waiting, self.flying = [], 0

    def add(self, copy, size):
        self.waiting.append((copy, size))

    def pump(self):
        while self.waiting and self.flying < IN_FLIGHT:
            copy, size = self.waiting.pop(0)
            copy.start()
            self.flying += size


class Operand:
    def __init__(self, ref, copy=None, queue=None):
        self.ref, self.copy, self.queue = ref, copy, queue
        if copy is not None:
            queue.add(copy, padded(ref))

    def get(self):
        if self.copy is not None:
            while any(copy is self.copy for copy, _ in self.queue.waiting):
                self.queue.flying = 0
                self.queue.pump()
            self.copy.wait()
            self.copy = None
            self.queue.flying -= padded(self.ref)
            self.queue.pump()
        return self.ref

    def __getitem__(self, index):
        return self.get()[index]


class Blocks:
    def __init__(self, operands):
        self.operands = operands

    def __getitem__(self, index):
        return self.operands[index[:2]][index[2:] + (slice(None),) * (3 - len(index[2:]))]


class Result:
    def __init__(self, ref, out=None, sems=None):
        self.ref, self.out, self.sems, self.copies = ref, out, sems, []

    def send(self, *index):
        if self.out is None:
            return
        view = (lambda r: r.at[index]) if index else (lambda r: r)
        copy = pltpu.make_async_copy(view(self.ref), view(self.out), self.sems.at[len(self.copies)])
        copy.start()
        self.copies.append(copy)


def project(basis, fields):
    parts = []
    for i, v in enumerate(fields):
        parts.append(lanes_join(nt(basis[i, 0], v), nt(basis[i, 1], v)))
    return jnp.concatenate(parts, axis=0)


def far_of(c, basis_re, basis_im):
    return tn(c.astype(BF16), basis_re) + tn(lanes_turn(c).astype(BF16), basis_im)


def expand(coeff_t, basis, i):
    rank = basis.shape[2]
    return far_of(coeff_t[i * rank : (i + 1) * rank], basis[i, 0], basis[i, 1])


def first_kernel(e_ref, k_ref, s_ref, t_ref, c_ref, pr_ref, fl_ref, nb_ref, out, mine, kept, left, right, keep, *, n):
    tc, tiles = pr_ref.ref.shape
    rank, tile = s_ref.ref.shape[2:]
    lanes = tc * rank
    rows = 2 * e_ref.ref.shape[1]
    columns = tiles * rank
    source = lax.broadcasted_iota(jnp.int32, (tiles, columns), 1) - rank * lax.broadcasted_iota(
        jnp.int32, (tiles, columns), 0
    )
    spread = jnp.where((source >= 0) & (source < rank), 1.0, 0.0).astype(F32)
    lane = lax.broadcasted_iota(jnp.int32, (rank, columns), 1).astype(F32)
    level = lane - rank * jnp.floor((lane + 0.5) / rank)
    top = jnp.maximum(level, lax.broadcasted_iota(jnp.int32, (rank, columns), 0).astype(F32))
    j = lax.broadcasted_iota(jnp.int32, (tc, tiles), 1)
    i = lax.broadcasted_iota(jnp.int32, (tc, tiles), 0) + lax.axis_index("tile") * tc
    distance = i - j
    distance = jnp.where(distance < 0, distance + tiles, distance)
    far = (fl_ref[...] == 1) & (distance != 0) & (distance != 1) & (distance != tiles - 1)
    limit = jnp.where(far, pr_ref[...], 0).astype(F32)
    wide = nn(limit, spread)
    mask = jnp.concatenate([jnp.where(top < wide[a : a + 1], 1.0, 0.0) for a in range(tc)], axis=0)
    m_re = (c_ref[0].astype(F32) * mask).astype(BF16)
    m_im = (c_ref[1].astype(F32) * mask).astype(BF16)
    kept.ref[0] = m_re
    kept.ref[1] = m_im
    kept.send()
    e = stacked(e_ref[...])
    coeff = project(s_ref.get(), [e[:, i * tile : (i + 1) * tile] for i in range(tc)]).astype(BF16)
    k = stacked(k_ref[...])
    proj = project(t_ref.get(), [k[:, i * tile : (i + 1) * tile] for i in range(tc)])
    back = tn(m_re, proj.astype(BF16)) + tn(m_im, lanes_turn(proj).astype(BF16))
    order = dealt(n)
    parts = [back[d * lanes : (d + 1) * lanes] for d in order]
    upper = bit_of(fold_bits(n)[0]) == 1
    sent = [coeff.astype(F32)]
    for low, high, at in zip(parts[: n // 2], parts[n // 2 :], range(n)):
        mine.ref[at] = jnp.where(upper, high, low)
        sent.append(pack(jnp.where(upper, low, high), rows))
    out.ref[...] = jnp.concatenate(sent, axis=0).astype(BF16)
    pair = lax.rem(lax.axis_index("src"), 2)
    part = k_ref.ref.shape[1] // 2
    own = stacked(k_ref.get()[:, pl.ds(pl.multiple_of(pair * part, part), part), :])
    sent = []
    for i, o in ((0, 0), (tc - 1, 2)):
        share = moved(own, nb_ref, tile, i, o).astype(BF16)
        rows_of = [t_ref[i, 0].astype(F32), t_ref[i, 1].astype(F32)]
        for at in range(0, columns, tile):
            end = min(columns, at + tile)
            for m in (m_re, m_im):
                piece = m[:, at:end].astype(F32)[i * rank : (i + 1) * rank]
                if end - at < tile:
                    piece = jnp.concatenate([piece, jnp.zeros((rank, tile - end + at), F32)], axis=1)
                rows_of.append(piece)
        factors = jnp.concatenate(rows_of, axis=0)
        half = factors.shape[0] // 2
        factors = jnp.where(pair == 0, factors[:half], factors[half:]).astype(BF16)
        sent.append(jnp.concatenate([share, factors], axis=0))
    put(left.ref, right.ref, *sent)


def deal_kernel(own_ref, other_ref, part_ref, *outs, n, fold):
    bits = fold_bits(n)
    rows = own_ref.ref.shape[1]
    count, lanes, width = part_ref.ref.shape
    deep = lanes * width // rows
    size = own_ref.ref.shape[0] - count * deep
    own, other = own_ref[...].astype(F32), other_ref[...].astype(F32)
    upper = bit_of(bits[fold]) == 1
    both = [jnp.where(upper, other[:size], own[:size]), jnp.where(upper, own[:size], other[:size])]
    sums = []
    for at in range(count):
        begin = size + at * deep
        sums.append(part_ref[at] + unpack(other[begin : begin + deep], lanes))
    if fold + 1 < len(bits):
        out, mine = outs
        upper = bit_of(bits[fold + 1]) == 1
        for low, high, at in zip(sums[: count // 2], sums[count // 2 :], range(count)):
            mine.ref[at] = jnp.where(upper, high, low)
            both.append(pack(jnp.where(upper, low, high), rows))
        out.ref[...] = jnp.concatenate(both, axis=0).astype(BF16)
        return
    *sent, mine, held = outs
    for at in range(4):
        held[at] = sums[at]
    here = bit_of(1) + 2 * bit_of(n // 2)
    mine.ref[...] = held[here]
    for k, out in zip((1, 2, 3), sent):
        block = pack(held[jnp.bitwise_xor(here, k)], rows)
        out.ref[...] = jnp.concatenate([*both, block], axis=0).astype(BF16)


def moved(k, nb_ref, tile, i, o):
    own = k[:, i * tile : (i + 1) * tile]
    return rows_join(nt(own, nb_ref[i, o, 0]), nt(own, nb_ref[i, o, 1]))


def near_of(fields, nb_ref, i, offsets):
    p = q = None
    for o in offsets:
        pp, qq = nn(fields[i + o - 1], nb_ref[i, o, 0]), nn(fields[i + o - 1], nb_ref[i, o, 1])
        p, q = (pp, qq) if p is None else (p + pp, q + qq)
    return rows_join(p, q)


def inside_kernel(nb_ref, v_ref, k_ref, start, loc, early, *, tile, tc):
    v, k = v_ref[...], stacked(k_ref[...])
    fields = {i: v[:, i * tile : (i + 1) * tile] for i in range(tc)}
    early.ref[...] = DAMPING * nt(k, v)
    for m in range(tc):
        cut = slice(m * tile, (m + 1) * tile)
        inner = [o for o in range(3) if m + o - 1 in fields]
        start.ref[:, cut] = fields[m].astype(F32) - DAMPING * near_of(fields, nb_ref, m, inner)
        total = None
        for o in range(3):
            if 0 <= m + 1 - o < tc:
                part = moved(k, nb_ref, tile, m + 1 - o, o)
                total = part if total is None else total + part
        loc.ref[:, cut] = total


def edge_kernel(start_ref, hl_ref, hr_ref, nb_ref, start, left, right, *, tile, tc):
    fields = dict(zip((-1, tc), sides(hl_ref[...], hr_ref[...])))
    ends = {}
    for i in range(tc):
        cut = slice(i * tile, (i + 1) * tile)
        value = start_ref[:, cut]
        for o in range(3):
            if i + o - 1 in fields:
                value = value - DAMPING * near_of(fields, nb_ref, i, [o])
        start.ref[:, cut] = value
        ends[i] = value.astype(BF16)
    put(left.ref, right.ref, ends[0], ends[tc - 1])


def second_near_kernel(*refs, tile, tc):
    fields = {i: refs[i][...] for i in range(tc)}
    hl_ref, hr_ref, edge_ref, bases_ref, nb_ref, e_ref, out = refs[tc:]
    for at, (i, h) in enumerate(zip((-1, tc), sides(hl_ref[...], hr_ref[...]))):
        far = far_of(edge_ref[at], bases_ref[at, 0], bases_ref[at, 1])
        fields[i] = (h.astype(F32) - DAMPING * far).astype(BF16)
    for i in range(tc):
        cut = slice(i * tile, (i + 1) * tile)
        near = near_of(fields, nb_ref, i, range(3))
        start = (1.0 - DAMPING) * fields[i].astype(F32) + DAMPING * stacked(e_ref[:, :, cut]).astype(F32)
        out.ref[:, cut] = start - DAMPING * near


def coupled_of(gathered, m_ref):
    turned = lanes_turn(gathered)
    coupled = nn(m_ref[0], gathered) + nn(m_ref[1], turned)
    return coupled.astype(BF16).astype(F32)


def middle_kernel(*refs, tile, tc):
    gots, refs = refs[:4], refs[4:]
    mine_ref, m_ref, t_ref, start_ref, s_ref, gl_ref, ol_ref, gr_ref, or_ref, early_ref, loc_ref, k_ref = refs[:12]
    tiles_out, (side, out, edge, bases, all_ref) = refs[12 : 12 + tc], refs[12 + tc :]
    lanes = m_ref.ref.shape[1]
    n = m_ref.ref.shape[2] // lanes
    rows = out.ref.shape[1]
    focal = k_ref.ref.shape[1]
    rank = t_ref.ref.shape[2]
    columns = n * lanes
    first = lax.rem(lax.axis_index("src"), 2) == 0

    def whole(own, other):
        own, other = own.astype(F32), other.astype(F32)
        low, high = jnp.where(first, own, other), jnp.where(first, other, own)
        half = focal // 2
        share = jnp.concatenate([low[:half], high[:half], low[half:focal], high[half:focal]], axis=0)
        factors = jnp.concatenate([low[focal:], high[focal:]], axis=0)
        basis = [factors[p * rank : (p + 1) * rank].astype(BF16) for p in range(2)]
        turns = []
        for p in range(2):
            pieces = [
                factors[(2 + 2 * c + p) * rank : (3 + 2 * c + p) * rank] for c in range(-(-columns // tile))
            ]
            turns.append((jnp.concatenate(pieces, axis=1) if len(pieces) > 1 else pieces[0])[:, :columns])
        return share, basis, turns

    (gl, gr), (ol, on_right) = sides(gl_ref[...], gr_ref[...]), sides(ol_ref[...], or_ref[...])
    share_l, basis_l, turns_l = whole(gl, ol)
    share_r, basis_r, turns_r = whole(gr, on_right)

    place(all_ref, gots, n, lanes)
    gathered = all_ref[...]
    stack = [
        jnp.concatenate([turns_l[p], m_ref[p].astype(F32), turns_r[p]], axis=0).astype(BF16) for p in range(2)
    ]
    coupled = (nn(stack[0], gathered) + nn(stack[1], lanes_turn(gathered))).astype(BF16).astype(F32)
    fields = []
    for i in range(tc):
        far = far_of(coupled[(i + 1) * rank : (i + 2) * rank], t_ref[i, 0], t_ref[i, 1])
        field = start_ref[:, i * tile : (i + 1) * tile] - DAMPING * far
        fields.append(field.astype(BF16))
        tiles_out[i].ref[...] = fields[i]
    edge.ref[0], edge.ref[1] = coupled[:rank], coupled[(tc + 1) * rank :]
    for p in range(2):
        bases.ref[0, p], bases.ref[1, p] = basis_l[p], basis_r[p]
    back = mine_ref[...]
    size = lanes << len(fold_bits(n))
    for got in gots[1:]:
        back = back + unpack(got[...][size:].astype(F32), lanes)
    back = back.astype(BF16).astype(F32)
    k = stacked(k_ref[...])
    p = early_ref[...]
    half = rows // 2
    for i in range(tc):
        cut = slice(i * tile, (i + 1) * tile)
        total = loc_ref[:, cut] + expand(back, s_ref.get(), i)
        if i == 0:
            total = total + share_l
        if i == tc - 1:
            total = total + share_r
        own = (-DAMPING * total).astype(BF16)
        side.ref[:, cut] = own
        side.send(slice(None), cut)
        p = p + (1.0 - DAMPING) * nt(k[:, cut], fields[i]) + nt(own, fields[i])
    half = rows // 2
    part = jnp.concatenate(
        [p[:focal, :half] - p[focal:, half:], p[:focal, half:] + p[focal:, :half]], axis=1
    ).astype(BF16)
    coeff = project(s_ref.get(), fields).astype(BF16)
    out.ref[:focal] = part
    out.ref[focal:] = coeff


def eye(n):
    return lax.broadcasted_iota(jnp.int32, (n, n), 0) == lax.broadcasted_iota(jnp.int32, (n, n), 1)


def pair_kernel(own_ref, other_ref, out, *, focal, bit):
    lanes = own_ref.ref.shape[0] - focal
    first = bit_of(bit) == 0
    own, other = own_ref[...].astype(F32), other_ref[...].astype(F32)
    out.ref[:focal] = (own[:focal] + other[:focal]).astype(BF16)
    out.ref[focal : focal + lanes] = jnp.where(first, own[focal:], other[focal:]).astype(BF16)
    out.ref[focal + lanes :] = jnp.where(first, other[focal:], own[focal:]).astype(BF16)


def sum_kernel(*refs, focal):
    gots, (foc, power) = refs[:-2], refs[-2:]
    half = foc.ref.shape[1] // 2
    total = gots[0][:focal].astype(F32)
    for got in gots[1:]:
        total = total + got[:focal].astype(F32)
    foc.ref[...] = total
    squares = total[:, :half] * total[:, :half] + total[:, half:] * total[:, half:]
    column = jnp.sum(squares, axis=1, keepdims=True)
    power.ref[...] = jnp.sum(jnp.where(eye(focal), column, 0.0), axis=0, keepdims=True)


def last_kernel(a_ref, b_ref, c_ref, d_ref, foc_ref, side_ref, k_ref, target_ref, owner_ref, adj, res, *, sources, scale):
    focal = foc_ref.ref.shape[0]
    half = foc_ref.ref.shape[1] // 2
    intensity = (a_ref[...] + b_ref[...]) + (c_ref[...] + d_ref[...])
    row = jnp.tanh(intensity / (2.0 * sources)) - target_ref[...]
    diagonal = eye(focal)
    column = jnp.sum(jnp.where(diagonal, row, 0.0), axis=1, keepdims=True)
    owner = jnp.sum(jnp.where(diagonal, owner_ref[...], 0), axis=1, keepdims=True)
    slots = res.ref.shape[1]
    slot = lax.broadcasted_iota(jnp.int32, (focal, slots), 1) + lax.axis_index("tile") * slots
    res.ref[...] = jnp.sum(jnp.where(owner == slot, column, 0.0), axis=0, keepdims=True)
    res.send()
    re = column * foc_ref[:, :half]
    im = -column * foc_ref[:, half:]
    w = jnp.concatenate([re, im], axis=1).astype(BF16)
    turned = jnp.concatenate([-im, re], axis=1).astype(BF16)
    both = jnp.concatenate([w, turned], axis=0)
    k = stacked(k_ref[...])
    width = k.shape[1]
    tile = width // 2
    for at in range(0, width, tile):
        cut = slice(at, at + tile)
        out = scale * (tn(both, k[:, cut]) + tn(both, side_ref[:, cut]))
        adj.ref[0, :, cut] = out[:half]
        adj.ref[1, :, cut] = out[half:]
        adj.send(slice(None), slice(None), cut)


def field_kernel(*refs, tile, tc, focal):
    gots, (m_ref, near_ref, t_ref, out) = refs[:-5], refs[-5:-1]
    all_ref = refs[-1]
    rows = all_ref.shape[1]
    half = rows // 2
    lanes = m_ref.ref.shape[1]
    place(all_ref, gots, all_ref.shape[0] // lanes, lanes, focal)
    coupled = coupled_of(all_ref[...], m_ref)
    for i in range(tc):
        cut = slice(i * tile, (i + 1) * tile)
        field = near_ref[:, cut] - DAMPING * expand(coupled, t_ref.get(), i)
        out.ref[0, :, cut] = field[:half]
        out.ref[1, :, cut] = field[half:]
        out.send(slice(None), slice(None), cut)


def edges_kernel(v_ref, near_ref, far_ref, sems):
    width, tile = v_ref.shape[1], near_ref.shape[1]
    odd = lax.rem(lax.axis_index("tile"), 2)
    copies = []
    for at, (ref, side) in enumerate(((near_ref, 1 - odd), (far_ref, odd))):
        begin = pl.multiple_of(side * (width - tile), 128)
        copies.append(pltpu.make_async_copy(v_ref.at[:, pl.ds(begin, tile)], ref, sems.at[at]))
    for copy in copies:
        copy.start()
    for copy in copies:
        copy.wait()


VM = pl.BlockSpec(memory_space=pltpu.VMEM)
FAR = pl.BlockSpec(memory_space=pltpu.HBM)


def in_hbm(x):
    return pltpu.with_memory_space_constraint(x, pltpu.HBM)


def padded(one):
    return math.prod(one.shape[:-1]) * -(-one.shape[-1] // 128) * 128 * jnp.dtype(one.dtype).itemsize


def call(kernel, outs, near, far=(), blocks=(), far_outs=(), extra=(), kept=None):
    far = [in_hbm(arg) for arg in far]
    held = [len(blocks) if arg.ndim == 5 and blocks else 0 for arg in far]
    scratch = [
        pltpu.VMEM((1, 128) if count and kept is not None else (count,) + arg.shape[2:] if count else arg.shape, arg.dtype)
        for arg, count in zip(far, held)
    ]
    scratch += [pltpu.VMEM(*outs[o]) for o in far_outs]
    scratch += [pltpu.VMEM(*one) for one in extra]
    taken = sum(padded(one) for one in scratch) + 3 * sum(padded(jax.ShapeDtypeStruct(s, d)) for s, d in outs)
    taken += 2 * sum(padded(one) for one in near)
    scratch += [pltpu.SemaphoreType.DMA((sum(count or 1 for count in held) + 1,))]
    scratch += [pltpu.SemaphoreType.DMA((len(far_outs) + 1, 8))]

    def run(*refs):
        refs = list(refs)
        close = [Operand(refs.pop(0)) for _ in near]
        queue = Queue()
        sources = [refs.pop(0) for _ in far]
        sinks = [refs.pop(0) for _ in outs]
        places = [refs.pop(0) for _ in far]
        stages = {o: refs.pop(0) for o in far_outs}
        more, (ins, ends) = refs[: len(extra)], refs[len(extra) :]
        operands, at = [], 0
        for source, place, count in zip(sources, places, held):
            if count:
                parts = {}
                for spot, block in enumerate(blocks):
                    target = place.at[spot] if kept is None else sinks[kept].at[block]
                    parts[block] = Operand(target, pltpu.make_async_copy(source.at[block], target, ins.at[at]), queue)
                    at += 1
                operands.append(Blocks(parts))
            else:
                operands.append(Operand(place, pltpu.make_async_copy(source, place, ins.at[at]), queue))
                at += 1
        queue.pump()
        results = []
        for o, sink in enumerate(sinks):
            results.append(Result(stages[o], sink, ends.at[far_outs.index(o)]) if o in stages else Result(sink))
        kernel(*close, *operands, *results, *more)
        for operand in operands:
            for one in operand.operands.values() if isinstance(operand, Blocks) else [operand]:
                one.get()
        for result in results:
            for copy in result.copies:
                copy.wait()

    return pl.pallas_call(
        run,
        out_shape=[
            pltpu.HBM(s, d) if o in far_outs else jax.ShapeDtypeStruct(s, d) for o, (s, d) in enumerate(outs)
        ],
        in_specs=[VM] * len(near) + [FAR] * len(far),
        out_specs=[FAR if o in far_outs else VM for o in range(len(outs))],
        scratch_shapes=scratch,
        compiler_params=pltpu.CompilerParams(vmem_limit_bytes=min(taken + (12 << 20), 60 * 1024 * 1024)),
    )(*near, *far)


def per_device(e, nb, sb, tb, coupling, pair_rank, far_link, fk, target, owner):
    tc, _, _, tile, _ = nb.shape
    rank = sb.shape[2]
    lanes = tc * rank
    half = e.shape[1]
    rows = 2 * half
    width = e.shape[2]
    tiles = pair_rank.shape[0]
    focal = target.shape[0]
    n = lax.axis_size("tile")
    groups = lax.axis_size("src")
    slots = focal // n
    edges = [(0, 0), (tc - 1, 2)]
    inside = [(i, o) for i in range(tc) for o in range(3) if (i, o) not in edges]
    sizes = dict(tile=tile, tc=tc)
    within = [(i, i ^ 1) for i in range(n)]
    across = [(i, (i - 1 + 2 * (i % 2)) % n) for i in range(n)]

    def exchange(near, far):
        return lax.ppermute(near, "tile", within), lax.ppermute(far, "tile", across)

    flat = stacked(e)
    el, er = pl.pallas_call(
        edges_kernel,
        out_shape=[jax.ShapeDtypeStruct((rows, tile), BF16)] * 2,
        in_specs=[FAR],
        out_specs=[VM, VM],
        scratch_shapes=[pltpu.SemaphoreType.DMA((2,))],
        compiler_params=pltpu.CompilerParams(vmem_limit_bytes=8 << 20),
        name="ends",
    )(in_hbm(flat))
    hl, hr = exchange(el, er)
    deep = lanes * 2 * focal // rows
    share = focal + rank * (1 + -(-tiles * rank // tile))
    send, part, masked, gl, gr, keep = call(
        functools.partial(first_kernel, n=n),
        [
            ((lanes + n // 2 * deep, rows), BF16),
            ((n // 2, lanes, 2 * focal), F32),
            ((2, lanes, tiles * rank), BF16),
            ((share, tile), BF16),
            ((share, tile), BF16),
            (nb.shape, BF16),
        ],
        [], [e, fk, sb, tb, jnp.swapaxes(coupling, 1, 2), pair_rank.T, far_link.T, nb],
        blocks=edges + inside, kept=5,
    )
    bits = fold_bits(n)
    for f, b in enumerate(bits):
        other = lax.ppermute(send, "tile", [(i, i ^ b) for i in range(n)])
        count = n >> (f + 1)
        if f + 1 < len(bits):
            outs = [
                ((lanes * (2 << f) + count // 2 * deep, rows), BF16),
                ((count // 2, lanes, 2 * focal), F32),
            ]
        else:
            outs = [((lanes * (2 << f) + deep, rows), BF16)] * 3 + [((lanes, 2 * focal), F32)]
        *sent, part = call(
            functools.partial(deal_kernel, n=n, fold=f), outs, [send, other, part],
            extra=[((4, lanes, 2 * focal), F32)] if f + 1 == len(bits) else [],
        )
        send = sent[0]
    got = [send] + [
        lax.ppermute(one, "tile", [(i, i ^ k) for i in range(n)]) for one, k in zip(sent, spread_offsets(n))
    ]
    from_left, from_right = exchange(gl, gr)
    start, loc, early = call(
        functools.partial(inside_kernel, **sizes),
        [((rows, width), F32), ((2 * focal, width), F32), ((2 * focal, rows), F32)],
        [keep], [flat, fk],
    )
    start, ql, qr = call(
        functools.partial(edge_kernel, **sizes),
        [((rows, width), F32), ((rows, tile), BF16), ((rows, tile), BF16)],
        [start, hl, hr, keep],
    )
    hl1, hr1 = exchange(ql, qr)
    swap = [(i, i ^ 1) for i in range(groups)]
    other_left, other_right = lax.ppermute(from_left, "src", swap), lax.ppermute(from_right, "src", swap)
    *f1, side, send1, edge, bases = call(
        functools.partial(middle_kernel, **sizes),
        [((rows, tile), BF16)] * tc
        + [
            ((2 * focal, width), BF16),
            ((focal + lanes, rows), BF16),
            ((2, rank, rows), F32),
            ((2, 2, rank, tile), BF16),
        ],
        [*got, part, masked, tb, start, sb, from_left, other_left, from_right, other_right, early, loc, fk],
        extra=[((n * lanes, rows), BF16)],
    )
    for f, b in enumerate(fold_bits(n)):
        other = lax.ppermute(send1, "tile", [(i, i ^ b) for i in range(n)])
        (send1,) = call(
            functools.partial(pair_kernel, focal=focal, bit=b),
            [((focal + (2 << f) * lanes, rows), BF16)], [send1, other],
        )
    gots = [send1]
    gots += [lax.ppermute(send1, "tile", [(i, i ^ k) for i in range(n)]) for k in spread_offsets(n)]
    (near1,) = call(
        functools.partial(second_near_kernel, **sizes), [((rows, width), F32)],
        [*f1, hl1, hr1, edge, bases, keep], [e],
    )
    foc, part = call(functools.partial(sum_kernel, focal=focal), [((focal, rows), F32), ((1, focal), F32)], gots)
    parts = [part] + [lax.ppermute(part, "src", [(i, i ^ k) for i in range(groups)]) for k in (1, 2, 3)]
    adjoint, residual = call(
        functools.partial(last_kernel, sources=half * groups, scale=(tiles * tile / focal) ** 0.5),
        [((2, half, width), F32), ((1, slots), F32)],
        [*parts, foc, side, fk], [target[None], owner[None]], far_outs=(0, 1),
    )
    (field,) = call(
        functools.partial(field_kernel, focal=focal, **sizes), [((2, half, width), F32)],
        [*gots, masked, near1, tb], far_outs=(0,), extra=[((n * lanes, rows), BF16)],
    )
    return field, residual[0], adjoint


def solution(mesh):
    return jax.shard_map(
        per_device,
        mesh=mesh,
        in_specs=(
            P(None, "src", "tile"),
            P("tile", None, None, None, None),
            P("tile", None, None, None),
            P("tile", None, None, None),
            P(None, None, "tile"),
            P(None, "tile"),
            P(None, "tile"),
            P(None, None, "tile"),
            P(),
            P(),
        ),
        out_specs=(P(None, "src", "tile"), P("tile"), P(None, "src", "tile")),
        check_vma=False,
    )
```
